32 devices in a mesh: cuts: 4 (over x, core), fiber: 8 (over z, y).
Axes of the slice: x: 2, y: 2, z: 4, core: 2. Of those that a mesh axis runs over, the one named last changes fastest.
Arguments:
- tile_vals: bfloat16 [131072, 128], P(('cuts', 'fiber')), may hold values from -6 to 6
- tile_count: int32 [131072], P(('cuts', 'fiber')), may hold values from 1 to 128
- tile_dest: int32 [131072, 1], P(('cuts', 'fiber')), may hold values from 0 to 3; in each aligned block of 4096 rows (0 to 4095, 4096 to 8191, ...) at most 2048 rows name the same one
- tile_row: int32 [131072], P(('cuts', 'fiber')), may hold values from 0 to 1023, as said below
- tile_block: int32 [131072], P(('cuts', 'fiber')), may hold values from 0 to 3
- tile_first: int32 [131072], P(('cuts', 'fiber')), may hold values from 0 to 255
- factor_one: bfloat16 [8192, 32], P(('cuts', 'fiber')), may hold values from -1.5 to 1.5
- factor_three: bfloat16 [4096, 32], P('fiber'), may hold values from -0.5 to 0.5
- factor_two: bfloat16 [4096, 32], P(('cuts', 'fiber')), may hold values from -0.09375 to 0.09375
Outputs:
- ttmc: bfloat16 [4096, 1024], P(('cuts', 'fiber'))
- projected: float32 [4096, 32], P(('cuts', 'fiber'))
The draws below stay inside these ranges and needn't reach their ends.
Inputs may be any that keep to these rules, and one draw needn't show every extreme that they name: `tile_dest`: among the tiles of one device, each index of cuts is named at most 2048 times, and exactly 2048 times by some. `tile_row`: among the tiles of one device, each block of 128 consecutive values (starting at multiples of 128) is taken exactly 512 times.
All inputs are finite; a program needn't handle non-finite values.
Results may differ from the reference program's by a relative error of at most 0.002.
Values may be sent and summed in bfloat16 or wider, within the bound.
A program may use at most 128 MiB of HBM per device.

```python
import math
import jax
import jax.numpy as jnp
import numpy as np
from jax import lax

R1 = 32
R2 = 32
R3 = 32
FIBER = 128
TILE_DEV = 4096
I2_DEV = 1024
I1_DEV = 256
KB_DEV = 4
CAP = 2048
ROWBLK = 128
TILES = 131072
I1 = 8192
I2 = 4096
I3 = 4096
N_CUTS = 4
N_FIBER = 8


def draw_tile_row(key, part):
    devices = TILES // TILE_DEV
    device_keys = jax.random.split(jax.random.fold_in(key, 7), devices)
    shuffled = jax.vmap(lambda single: jax.random.permutation(single, TILE_DEV))(device_keys)
    row_owner = shuffled % (I2_DEV // ROWBLK)
    within = jax.random.randint(jax.random.fold_in(key, 11), (devices, TILE_DEV), 0, ROWBLK)
    return (row_owner * ROWBLK + within).reshape(TILES).astype(jnp.int32)


def plant(result, key, smallest, largest):
    extent = result.shape
    spot = [jax.random.randint(jax.random.fold_in(key, axis), (), 0, extent[axis]) for axis in range(len(extent))]
    result = result.at[tuple(spot)].set(smallest)
    longest = extent.index(max(extent))
    spot[longest] = (spot[longest] + 1) % extent[longest]
    return result.at[tuple(spot)].set(largest)


def level_of(key, shape, cuts, least, largest):
    loudness = 1.0
    for position, parts in cuts:
        heights = jax.random.uniform(jax.random.fold_in(jax.random.fold_in(key, 6), position), (parts,), jnp.float32, least / len(cuts), largest / len(cuts))
        loudness = loudness * jnp.repeat(jnp.exp(heights), shape[position] // parts).reshape((-1,) + (1,) * (len(shape) - 1 - position))
    return loudness


def shared_out(stream_key, own, number, rows, number_of, top, reach, slope):
    ranking = jax.random.permutation(stream_key, number_of)
    packed, usual = portions_of(number_of, rows * top, reach, slope, True), portions_of(number_of, rows * top, reach, slope, False)
    places = jnp.arange(number_of)

    def named(lengths, offset_by):
        used = int((lengths > 0).sum())
        fixed = max(1, used // 4)
        passed = fixed + (places - fixed + offset_by * (used - fixed)) % max(1, number_of - fixed)
        return jnp.zeros((number_of,), jnp.int32).at[ranking[jnp.where(places < fixed, places, passed)]].set(jnp.asarray(lengths, jnp.int32))

    lengths = jnp.where(number % 4 == 0, named(packed, number // 4), named(usual, number - number // 4 - 1))
    mixed = jax.random.permutation(jax.random.fold_in(own, 3), number_of)
    donor, sink = mixed[0:number_of // 2 * 2:2], mixed[1:number_of // 2 * 2:2]
    margin = jnp.minimum(lengths[donor] - 1, reach - lengths[sink]) // 2
    margin = jnp.where((donor == ranking[0]) | (sink == ranking[0]) | (lengths[sink] == 0), 0, jnp.maximum(margin, 0))
    passed = jax.random.randint(jax.random.fold_in(own, 4), (number_of // 2,), 0, 1 << 20) % (margin + 1)
    lengths = lengths.at[donor].add(-passed).at[sink].add(passed)
    labels = jnp.searchsorted(jnp.cumsum(lengths), jnp.arange(rows * top), side="right").astype(jnp.int32)
    table = labels.reshape(top, rows).T
    table = table[jax.random.permutation(jax.random.fold_in(own, 1), rows)]
    offset_by = jax.random.randint(jax.random.fold_in(own, 2), (rows, 1), 0, top)
    return jnp.take_along_axis(table, (jnp.arange(top)[None, :] + offset_by) % top, axis=1)


def portions_of(count, total, limit, slope, full):
    loads = [(1 << 20) // math.isqrt(grade ** slope) + 1 for grade in range(1, count + 1)]
    largest = limit if full else min(limit, max(-(-total // count), total * loads[0] // sum(loads)))
    least = 1 if total - largest >= count - 1 else 0
    given, spare = [largest] + [least] * (count - 1), total - largest - least * (count - 1)
    while spare > 0:
        movable = [i for i in range(1, count) if given[i] < largest] or [i for i in range(1, count) if given[i] < limit]
        whole, left = sum([loads[i] for i in movable]), spare
        for i in movable:
            more = min(limit - given[i], max(1, left * loads[i] // whole), spare)
            given[i] = given[i] + more
            spare = spare - more
    return np.array(given)


def centred(own_key, dims, deviation, limit, cuts=(), held_as=jnp.bfloat16):
    gain = level_of(own_key, dims, cuts, -0.22, 0.18) if cuts else 1.0
    drawn = jax.random.normal(own_key, dims, jnp.float32) * deviation * gain
    return jnp.minimum(jnp.maximum(drawn, -limit), limit).astype(held_as)


def setup_inputs(seed: int = 0) -> dict:
    key_of = jax.random.split(jax.random.key(seed), 10)
    tile_vals = centred(key_of[0], (TILES, FIBER), 1.0, 6.0, ((0, 32),))
    tile_count = plant(jax.random.randint(key_of[1], (TILES,), 1, FIBER + 1), jax.random.fold_in(key_of[1], 1), 1, FIBER).astype(jnp.int32)
    tile_dest_keys = jax.random.split(jax.random.fold_in(key_of[2], 1), TILES // TILE_DEV)
    tile_dest_turns = jax.random.permutation(jax.random.fold_in(key_of[2], 3), TILES // TILE_DEV)
    tile_dest = jax.vmap(lambda own, number: shared_out(jax.random.fold_in(key_of[2], 2), own, number, TILE_DEV, N_CUTS, 1, CAP, 2))(tile_dest_keys, tile_dest_turns).reshape((TILES, 1))
    tile_row = draw_tile_row(jax.random.fold_in(key_of[9], 71), 0)
    tile_block = plant(jax.random.randint(key_of[4], (TILES,), 0, KB_DEV), jax.random.fold_in(key_of[4], 1), 0, KB_DEV - 1).astype(jnp.int32)
    tile_first = plant(jax.random.randint(key_of[5], (TILES,), 0, I1_DEV), jax.random.fold_in(key_of[5], 1), 0, I1_DEV - 1).astype(jnp.int32)
    factor_one = centred(key_of[6], (I1, R1), 0.25, 1.5, ((0, 32),))
    factor_three = centred(key_of[7], (I3, R3), FIBER ** -0.5, 0.5, ((0, 8),))
    factor_two = centred(key_of[8], (I2, R2), I2 ** -0.5, 0.09375, ((0, 32),))
    return {"tile_vals": tile_vals, "tile_count": tile_count, "tile_dest": tile_dest, "tile_row": tile_row, "tile_block": tile_block, "tile_first": tile_first, "factor_one": factor_one, "factor_three": factor_three, "factor_two": factor_two}


def reference(tile_vals, tile_count, tile_dest, tile_row, tile_block, tile_first, factor_one, factor_three, factor_two):
    positions = jnp.arange(FIBER, dtype=jnp.int32)
    total_rows = I2_DEV * N_CUTS

    def step(acc, device):
        start = device * TILE_DEV
        vals = lax.dynamic_slice_in_dim(tile_vals, start, TILE_DEV, 0)
        counts = lax.dynamic_slice_in_dim(tile_count, start, TILE_DEV, 0)
        dests = lax.dynamic_slice_in_dim(tile_dest, start, TILE_DEV, 0)[:, 0]
        rows_in = lax.dynamic_slice_in_dim(tile_row, start, TILE_DEV, 0)
        blocks = lax.dynamic_slice_in_dim(tile_block, start, TILE_DEV, 0)
        firsts = lax.dynamic_slice_in_dim(tile_first, start, TILE_DEV, 0)
        masked = jnp.where(positions[None, :] < counts[:, None], vals, jnp.zeros_like(vals))
        fib = device % N_FIBER
        third = lax.dynamic_slice_in_dim(factor_three, fib * (KB_DEV * FIBER), KB_DEV * FIBER, 0)
        third = third.reshape(KB_DEV, FIBER, R3)
        picked = third[blocks].astype(jnp.float32)
        proj = jnp.einsum('tk,tkr->tr', masked.astype(jnp.float32), picked)
        first_rows = lax.dynamic_slice_in_dim(factor_one, device * I1_DEV, I1_DEV, 0)[firsts].astype(jnp.float32)
        kron = (first_rows[:, :, None] * proj[:, None, :]).reshape(TILE_DEV, R1 * R3)
        target = (dests * I2_DEV + rows_in).astype(jnp.int32)
        return acc + jax.ops.segment_sum(kron, target, num_segments=total_rows), None

    start_acc = jnp.zeros((total_rows, R1 * R3), jnp.float32)
    rows, _ = lax.scan(step, start_acc, jnp.arange(N_CUTS * N_FIBER, dtype=jnp.int32))
    ttmc = rows.astype(jnp.bfloat16)
    gram = lax.dot_general(ttmc, factor_two, (((0,), (0,)), ((), ())), preferred_element_type=jnp.float32)
    gram_b = gram.astype(jnp.bfloat16)
    projected = jnp.dot(ttmc, gram_b, preferred_element_type=jnp.float32) / 32.0
    return ttmc, projected
```

```python
import functools

import jax
import jax.numpy as jnp
from jax import lax
from jax.experimental import pallas as pl
from jax.experimental.pallas import tpu as pltpu
from jax.sharding import PartitionSpec as P

FIBER = 128
CHUNK = 512
LANES = 128
GROWS = 16
MESH = pl.DeviceIdType.MESH
NT = (((1,), (1,)), ((), ()))


def onehot(count, row, dtype=jnp.bfloat16):
    spots = lax.broadcasted_iota(jnp.int32, (count, row.shape[1]), 0).astype(row.dtype)
    return jnp.where(spots == row, 1.0, 0.0).astype(dtype)


def dot_nt(a, b):
    return lax.dot_general(a, b, NT, preferred_element_type=jnp.float32)


def kernel(
    nc,
    nf,
    vals_hbm,
    count_ref,
    dest_ref,
    row_ref,
    block_ref,
    first_ref,
    f1_ref,
    f2_ref,
    f3_ref,
    ttmc_ref,
    out_ref,
    vals,
    slots,
    spread,
    placed,
    send,
    send_key,
    got,
    got_key,
    f1s,
    got_f1,
    got_f1x,
    f2all,
    acc,
    sib,
    gram,
    grecv,
    gown,
    gall,
    back,
    gfull,
    rows_out,
    rows_in,
    v_sem,
    a2a_send,
    a2a_recv,
    x_send,
    x_recv,
    f2_send,
    f2_recv,
    sib_send,
    sib_recv,
    row_send,
    row_recv,
    g_send,
    g_recv,
    b_send,
    b_recv,
):
    tiles = vals.shape[0]
    r1, i1 = f1_ref.shape
    r2, br = f2_ref.shape
    r3 = f3_ref.shape[0]
    blocks = f3_ref.shape[1] // FIBER
    cap = send.shape[2]
    chunks = tiles // CHUNK
    width = r1 * r3
    nx = nc // 2
    per_x = r1 // nx
    quarter = width // nc
    feats = placed.shape[1]
    ndev = nc * nf
    parts = quarter // LANES
    per_part = r2 // GROWS
    pieces = parts * per_part
    stride = (nf // 2) // pieces
    q = lax.axis_index("cuts")
    f = lax.axis_index("fiber")
    x = q // 2
    c = q % 2
    me = q * nf + f

    def vals_copy(k):
        rows = pl.ds(k * CHUNK, CHUNK)
        return pltpu.make_async_copy(vals_hbm.at[rows], vals.at[rows], v_sem.at[k])

    for k in range(chunks):
        vals_copy(k).start()

    barrier = pltpu.get_barrier_semaphore()

    @pl.loop(1, ndev)
    def _(k):
        other = lax.rem(me + k, ndev)
        pl.semaphore_signal(
            barrier, inc=1, device_id=(other // nf, lax.rem(other, nf)), device_id_type=MESH
        )

    def a2a_copy(what, j):
        source = (send.at[j], send_key.at[j], f1s)[what]
        target = (got.at[0, j], got_key.at[0, j], got_f1.at[j])[what]
        return pltpu.make_async_remote_copy(
            src_ref=source,
            dst_ref=target,
            send_sem=a2a_send.at[what, j],
            recv_sem=a2a_recv.at[what, j],
            device_id=(q, lax.rem(f + j, nf)),
            device_id_type=MESH,
        )

    def x_copy(what, dx, j):
        there = lax.rem(x + dx, nx)
        source = (got.at[0, j], got_key.at[0, j], got_f1.at[j, there])[what]
        target = (got.at[dx, j], got_key.at[dx, j], got_f1x.at[dx, j])[what]
        return pltpu.make_async_remote_copy(
            src_ref=source,
            dst_ref=target,
            send_sem=x_send.at[what, dx, j],
            recv_sem=x_recv.at[what, dx, j],
            device_id=(there * 2 + c, f),
            device_id_type=MESH,
        )

    def f2_copy(dq):
        return pltpu.make_async_remote_copy(
            src_ref=f2all.at[q],
            dst_ref=f2all.at[q],
            send_sem=f2_send.at[dq],
            recv_sem=f2_recv.at[dq],
            device_id=(lax.rem(q + dq, nc), f),
            device_id_type=MESH,
        )

    for k in range(nx):
        f1s[k] = f1_ref[k * per_x : (k + 1) * per_x, :]
        got_f1[0, k] = f1_ref[k * per_x : (k + 1) * per_x, :]
    f2all[q] = f2_ref[...]

    groups = lax.broadcasted_iota(jnp.int32, (nf, tiles), 0)
    owner = row_ref[...] // br
    member = jnp.where(groups == owner, 1.0, 0.0)
    stacked = jnp.concatenate(
        [member[:, k * CHUNK : (k + 1) * CHUNK] for k in range(chunks)], axis=0
    )
    early = lax.broadcasted_iota(jnp.int32, (CHUNK, CHUNK), 0)
    late = lax.broadcasted_iota(jnp.int32, (CHUNK, CHUNK), 1)
    before = jnp.dot(
        stacked.astype(jnp.bfloat16),
        jnp.where(early < late, 1.0, 0.0).astype(jnp.bfloat16),
        preferred_element_type=jnp.float32,
    )
    diagonal = (
        lax.broadcasted_iota(jnp.int32, (FIBER, FIBER), 0)
        == lax.broadcasted_iota(jnp.int32, (FIBER, FIBER), 1)
    )
    eye = jnp.where(diagonal, 1.0, 0.0).astype(jnp.bfloat16)
    table = jnp.concatenate(
        [f3_ref[:, k * FIBER : (k + 1) * FIBER] for k in range(blocks)], axis=0
    )
    position = lax.broadcasted_iota(jnp.int32, (FIBER, CHUNK), 0)
    kind = lax.broadcasted_iota(jnp.int32, (16, CHUNK), 0)
    carry = jnp.zeros((nf, 1), jnp.float32)
    for k in range(chunks):
        cols = slice(k * CHUNK, (k + 1) * CHUNK)
        mem = member[:, cols]
        rank = jnp.sum(mem * (before[k * nf : (k + 1) * nf] + carry), axis=0, keepdims=True)
        carry = carry + jnp.sum(mem, axis=1, keepdims=True)
        slots[:, cols] = onehot(cap, rank)
        marks = jnp.where(
            kind == 0,
            dest_ref[:, cols],
            jnp.where(
                kind == 1,
                row_ref[:, cols] % br,
                jnp.where(kind == 2, first_ref[:, cols], 0),
            ),
        )
        vals_copy(k).wait()
        turned = dot_nt(eye, vals[cols, :])
        masked = jnp.where(position < count_ref[:, cols], turned, 0.0).astype(jnp.bfloat16)
        every = jnp.dot(table, masked, preferred_element_type=jnp.float32)
        value = every[0:r3]
        for b in range(1, blocks):
            value = jnp.where(block_ref[:, cols] == b, every[b * r3 : (b + 1) * r3], value)
        high = value.astype(jnp.bfloat16)
        low = (value - high.astype(jnp.float32)).astype(jnp.bfloat16)
        data = jnp.concatenate([high, low, marks.astype(jnp.float32).astype(jnp.bfloat16)], axis=0)
        for g in range(nf):
            spread[g * feats : (g + 1) * feats, cols] = data * mem[g : g + 1].astype(jnp.bfloat16)

    together = dot_nt(spread[...], slots[...])
    for g in range(nf):
        placed[g] = together[g * feats : (g + 1) * feats]

    @pl.loop(0, nf)
    def _(j):
        block = placed[lax.rem(f + j, nf)]
        value = block[0:r3] + block[r3 : 2 * r3]
        top = jnp.max(jnp.abs(value), axis=0, keepdims=True)
        scale = jnp.maximum(top, 1e-32) * (1.0 / 32512.0)
        coded = jnp.floor(value * (1.0 / scale) + 0.5).astype(jnp.int32).astype(jnp.int16)
        marks = block[2 * r3 : 2 * r3 + 3]
        key = (marks[0:1] * br + marks[1:2]) * i1 + marks[2:3]

        @pl.when(j != 0)
        def _():
            send[j] = coded
            send_key[j, 0:1] = key
            send_key[j, 1:2] = scale

        @pl.when(j == 0)
        def _():
            got[0, 0] = coded
            got_key[0, 0, 0:1] = key
            got_key[0, 0, 1:2] = scale

    pl.semaphore_wait(barrier, ndev - 1)

    def step_of(pair):
        late = (pair + nf // 2 - 1) // (nf // 2)
        return late * (2 + lax.rem(2 * (pair - 1) + nf // 2 - 2 + nf - 2, nf - 2))

    def turn(i):
        return step_of(i // 2) + lax.rem(i, 2)

    def forward(j):
        for dx in range(1, nx):
            for what in (2, 1, 0):
                x_copy(what, dx, j).start()

    @pl.loop(1, nf)
    def _(i):
        for what in (2, 1, 0):
            a2a_copy(what, turn(i)).start()

    forward(0)
    for dq in range(1, nc):
        f2_copy(dq).start()

    def terms(dx, j):
        key = got_key[dx, j, 0:1]
        target = jnp.floor(key * (1.0 / i1))
        slab = got_f1[j, x] if dx == 0 else got_f1x[dx, j]
        fr = jnp.dot(slab, onehot(i1, key - target * i1), preferred_element_type=jnp.float32)
        sel = onehot(nc * br, target)
        value = got[dx, j].astype(jnp.int32).astype(jnp.float32) * got_key[dx, j, 1:2]
        prod = jnp.concatenate([fr[a : a + 1] * value for a in range(per_x)], axis=0)
        high = prod.astype(jnp.bfloat16)
        low = (prod - high.astype(jnp.float32)).astype(jnp.bfloat16)
        return [high, low], [sel, sel]

    def arrive(which):
        left, right = [], []
        for dx, j in which:
            more_left, more_right = terms(dx, j)
            left += more_left
            right += more_right
        return dot_nt(jnp.concatenate(left, axis=1), jnp.concatenate(right, axis=1))

    acc[...] = arrive([(0, 0)])

    @pl.loop(1, nf)
    def _(i):
        j = turn(i)
        for what in (2, 1, 0):
            a2a_copy(what, j).wait()
        forward(j)
        prior = turn(i - 1)
        for dx in range(1, nx):
            for what in (2, 1, 0):
                x_copy(what, dx, prior).wait()
        acc[...] += arrive([(0, j)] + [(dx, prior) for dx in range(1, nx)])

    last = turn(nf - 1)
    for dx in range(1, nx):
        for what in (2, 1, 0):
            x_copy(what, dx, last).wait()
    acc[...] += arrive([(dx, last) for dx in range(1, nx)])

    def sib_copy(k):
        return pltpu.make_async_remote_copy(
            src_ref=acc.at[pl.ds((1 - c) * quarter + k * LANES, LANES)],
            dst_ref=sib.at[pl.ds(k * LANES, LANES)],
            send_sem=sib_send.at[k],
            recv_sem=sib_recv.at[k],
            device_id=(x * 2 + 1 - c, f),
            device_id_type=MESH,
        )

    def gram_copy(p, to):
        return pltpu.make_async_remote_copy(
            src_ref=gram.at[p],
            dst_ref=grecv.at[f],
            send_sem=g_send,
            recv_sem=g_recv,
            device_id=(q, to),
            device_id_type=MESH,
        )

    def row_copy(dq):
        there = lax.rem(q + dq, nc)
        return pltpu.make_async_remote_copy(
            src_ref=rows_out.at[there],
            dst_ref=rows_in.at[q],
            send_sem=row_send.at[dq],
            recv_sem=row_recv.at[dq],
            device_id=(there, f),
            device_id_type=MESH,
        )

    def back_copy(k, slot):
        to = lax.rem(me + k, ndev)
        return pltpu.make_async_remote_copy(
            src_ref=gown,
            dst_ref=gall.at[slot],
            send_sem=b_send,
            recv_sem=b_recv,
            device_id=(to // nf, lax.rem(to, nf)),
            device_id_type=MESH,
        )

    def drain(ref, count, sem):
        pltpu.make_async_copy(ref.at[pl.ds(0, count)], ref.at[pl.ds(0, count)], sem).wait()

    for k in range(parts):
        sib_copy(k).start()
    for dq in range(1, nc):
        f2_copy(dq).wait()
    second = jnp.concatenate([f2all[k] for k in range(nc)], axis=1)
    totals = []
    for k in range(parts):
        sib_copy(k).wait()
        total = acc[pl.ds(c * quarter + k * LANES, LANES), :] + sib[k * LANES : (k + 1) * LANES, :]
        totals.append(total)
        local = dot_nt(second, total.astype(jnp.bfloat16))
        for h in range(per_part):
            p = k * per_part + h
            to = nf // 4 + p * stride
            piece = local[h * GROWS : (h + 1) * GROWS]
            gram[p] = piece

            @pl.when(f != to)
            def _():
                gram_copy(p, to).start()

            @pl.when(f == to)
            def _():
                grecv[f] = piece

    for k in range(parts):
        upright = totals[k].T.astype(jnp.bfloat16)
        for d in range(nc):
            rows_out[d, :, k * LANES : (k + 1) * LANES] = upright[d * br : (d + 1) * br]
    for dq in range(1, nc):
        row_copy(dq).start()

    shifted = lax.rem(f + nf - nf // 4, nf)
    mine = shifted // stride
    owns = jnp.logical_and(shifted < pieces * stride, lax.rem(shifted, stride) == 0)

    @pl.when(owns)
    def _():
        drain(grecv, nf - 1, g_recv)
        whole = jnp.sum(grecv[...], axis=0).astype(jnp.bfloat16)
        slot = q * pieces + mine
        gown[...] = whole
        gall[slot] = whole

        @pl.loop(1, ndev)
        def _(k):
            back_copy(k, slot).start()

    rows_in[q] = rows_out[q]
    for dq in range(1, nc):
        row_copy(dq).wait()
    for d in range(nc):
        ttmc_ref[:, d * quarter : (d + 1) * quarter] = rows_in[d]

    @pl.when(owns)
    def _():
        drain(gall, nc * pieces - 1, b_recv)

    @pl.when(jnp.logical_not(owns))
    def _():
        drain(gall, nc * pieces, b_recv)

    for d in range(nc):
        for p in range(pieces):
            k, h = p // per_part, p % per_part
            start = d * quarter + k * LANES
            gfull[h * GROWS : (h + 1) * GROWS, start : start + LANES] = gall[d * pieces + p]
    out_ref[...] = dot_nt(gfull[...], ttmc_ref[...]) / 32.0

    @pl.when(owns)
    def _():
        drain(gram, pieces - 1, g_send)
        drain(back, ndev - 1, b_send)

    @pl.when(jnp.logical_not(owns))
    def _():
        drain(gram, pieces, g_send)


def body(
    tile_vals,
    tile_count,
    tile_dest,
    tile_row,
    tile_block,
    tile_first,
    factor_one,
    factor_three,
    factor_two,
):
    nc = lax.axis_size("cuts")
    nf = lax.axis_size("fiber")
    tiles = tile_vals.shape[0]
    r1, r2, r3 = factor_one.shape[1], factor_two.shape[1], factor_three.shape[1]
    br = factor_two.shape[0]
    cap = tiles // nf
    width = r1 * r3
    nx = nc // 2
    i1 = factor_one.shape[0]
    feats = 2 * r3 + 16
    quarter = width // nc
    parts = quarter // LANES
    pieces = parts * (r2 // GROWS)
    vmem = pl.BlockSpec(memory_space=pltpu.VMEM)
    bf16, f32, i16 = jnp.bfloat16, jnp.float32, jnp.int16
    dma = pltpu.SemaphoreType.DMA
    ttmc, projected = pl.pallas_call(
        functools.partial(kernel, nc, nf),
        out_shape=(
            jax.ShapeDtypeStruct((br, width), bf16),
            jax.ShapeDtypeStruct((r2, br), f32),
        ),
        in_specs=[pl.BlockSpec(memory_space=pl.ANY)] + [vmem] * 8,
        out_specs=(vmem, vmem),
        scratch_shapes=[
            pltpu.VMEM((tiles, FIBER), bf16),
            pltpu.VMEM((cap, tiles), bf16),
            pltpu.VMEM((nf * feats, tiles), bf16),
            pltpu.VMEM((nf, feats, cap), f32),
            pltpu.VMEM((nf, r3, cap), i16),
            pltpu.VMEM((nf, 2, cap), f32),
            pltpu.VMEM((nx, nf, r3, cap), i16),
            pltpu.VMEM((nx, nf, 2, cap), f32),
            pltpu.VMEM((nx, r1 // nx, i1), bf16),
            pltpu.VMEM((nf, nx, r1 // nx, i1), bf16),
            pltpu.VMEM((nx, nf, r1 // nx, i1), bf16),
            pltpu.VMEM((nc, r2, br), bf16),
            pltpu.VMEM((width // nx, nc * br), f32),
            pltpu.VMEM((quarter, nc * br), f32),
            pltpu.VMEM((pieces, GROWS, LANES), f32),
            pltpu.VMEM((nf, GROWS, LANES), f32),
            pltpu.VMEM((GROWS, LANES), bf16),
            pltpu.VMEM((nc * pieces, GROWS, LANES), bf16),
            pltpu.VMEM((nc * nf, GROWS, LANES), bf16),
            pltpu.VMEM((r2, width), bf16),
            pltpu.VMEM((nc, br, quarter), bf16),
            pltpu.VMEM((nc, br, quarter), bf16),
            dma((tiles // CHUNK,)),
            dma((3, nf)),
            dma((3, nf)),
            dma((3, nx, nf)),
            dma((3, nx, nf)),
            dma((nc,)),
            dma((nc,)),
            dma((parts,)),
            dma((parts,)),
            dma((nc,)),
            dma((nc,)),
            dma,
            dma,
            dma,
            dma,
        ],
        compiler_params=pltpu.CompilerParams(
            collective_id=0, has_side_effects=True, vmem_limit_bytes=60 * 1024 * 1024
        ),
    )(
        tile_vals,
        tile_count.reshape(1, tiles),
        tile_dest.reshape(1, tiles),
        tile_row.reshape(1, tiles),
        tile_block.reshape(1, tiles),
        tile_first.reshape(1, tiles),
        factor_one.T,
        factor_two.T,
        factor_three.T,
    )
    return ttmc, projected.T


def solution(mesh):
    in_specs = (
        P(("cuts", "fiber"), None),
        P(("cuts", "fiber")),
        P(("cuts", "fiber"), None),
        P(("cuts", "fiber")),
        P(("cuts", "fiber")),
        P(("cuts", "fiber")),
        P(("cuts", "fiber"), None),
        P("fiber", None),
        P(("cuts", "fiber"), None),
    )
    out_specs = (P(("cuts", "fiber"), None), P(("cuts", "fiber"), None))
    return jax.shard_map(body, mesh=mesh, in_specs=in_specs, out_specs=out_specs, check_vma=False)
```

```python
import functools

import jax
import jax.numpy as jnp
from jax import lax
from jax.experimental import pallas as pl
from jax.experimental.pallas import tpu as pltpu
from jax.sharding import PartitionSpec as P

FIBER = 128
CHUNK = 512
LANES = 128
GROWS = 16
SPLIT = 2
MESH = pl.DeviceIdType.MESH
NT = (((1,), (1,)), ((), ()))


def onehot(count, row, dtype=jnp.bfloat16):
    spots = lax.broadcasted_iota(jnp.int32, (count, row.shape[1]), 0).astype(row.dtype)
    return jnp.where(spots == row, 1.0, 0.0).astype(dtype)


def dot_nt(a, b):
    return lax.dot_general(a, b, NT, preferred_element_type=jnp.float32)


def kernel(
    nc,
    nf,
    vals_hbm,
    count_ref,
    dest_ref,
    row_ref,
    block_ref,
    first_ref,
    f1_ref,
    f2_ref,
    f3_ref,
    ttmc_ref,
    out_ref,
    vals,
    slots,
    spread,
    send,
    send_key,
    got,
    got_key,
    f1s,
    got_f1,
    got_f1x,
    f2all,
    acc,
    sib,
    gram,
    grecv,
    gown,
    gall,
    back,
    gfull,
    rows_out,
    rows_in,
    v_sem,
    a2a_send,
    a2a_recv,
    x_send,
    x_recv,
    f2_send,
    f2_recv,
    sib_send,
    sib_recv,
    row_send,
    row_recv,
    g_send,
    g_recv,
    b_send,
    b_recv,
):
    tiles = vals.shape[0]
    r1, i1 = f1_ref.shape
    r2, br = f2_ref.shape
    r3 = f3_ref.shape[0]
    blocks = f3_ref.shape[1] // FIBER
    cap = send.shape[2]
    chunks = tiles // CHUNK
    width = r1 * r3
    nx = nc // 2
    per_x = r1 // nx
    quarter = width // nc
    feats = spread.shape[0] // nf
    ndev = nc * nf
    parts = quarter // LANES
    per_part = r2 // GROWS
    pieces = parts * per_part
    stride = (nf // 2) // pieces
    q = lax.axis_index("cuts")
    f = lax.axis_index("fiber")
    x = q // 2
    c = q % 2
    me = q * nf + f

    def vals_copy(k):
        rows = pl.ds(k * CHUNK, CHUNK)
        return pltpu.make_async_copy(vals_hbm.at[rows], vals.at[rows], v_sem.at[k])

    for k in range(chunks):
        vals_copy(k).start()

    barrier = pltpu.get_barrier_semaphore()

    @pl.loop(1, ndev)
    def _(k):
        other = lax.rem(me + k, ndev)
        pl.semaphore_signal(
            barrier, inc=1, device_id=(other // nf, lax.rem(other, nf)), device_id_type=MESH
        )

    def a2a_copy(what, j):
        source = (send.at[j], send_key.at[j], f1s)[what]
        target = (got.at[0, j], got_key.at[0, j], got_f1.at[j])[what]
        return pltpu.make_async_remote_copy(
            src_ref=source,
            dst_ref=target,
            send_sem=a2a_send.at[what, j],
            recv_sem=a2a_recv.at[what, j],
            device_id=(q, lax.rem(f + j, nf)),
            device_id_type=MESH,
        )

    def x_copy(what, dx, j):
        there = lax.rem(x + dx, nx)
        source = (got.at[0, j], got_key.at[0, j], got_f1.at[j, there])[what]
        target = (got.at[dx, j], got_key.at[dx, j], got_f1x.at[dx, j])[what]
        return pltpu.make_async_remote_copy(
            src_ref=source,
            dst_ref=target,
            send_sem=x_send.at[what, dx, j],
            recv_sem=x_recv.at[what, dx, j],
            device_id=(there * 2 + c, f),
            device_id_type=MESH,
        )

    def f2_copy(dq):
        return pltpu.make_async_remote_copy(
            src_ref=f2all.at[q],
            dst_ref=f2all.at[q],
            send_sem=f2_send.at[dq],
            recv_sem=f2_recv.at[dq],
            device_id=(lax.rem(q + dq, nc), f),
            device_id_type=MESH,
        )

    for k in range(nx):
        f1s[k] = f1_ref[k * per_x : (k + 1) * per_x, :]
        got_f1[0, k] = f1_ref[k * per_x : (k + 1) * per_x, :]
    f2all[q] = f2_ref[...]

    groups = lax.rem(lax.broadcasted_iota(jnp.int32, (nf, tiles), 0) + f, nf)
    owner = row_ref[...] // br
    member = jnp.where(groups == owner, 1.0, 0.0)
    stacked = jnp.concatenate(
        [member[:, k * CHUNK : (k + 1) * CHUNK] for k in range(chunks)], axis=0
    )
    early = lax.broadcasted_iota(jnp.int32, (CHUNK, CHUNK), 0)
    late = lax.broadcasted_iota(jnp.int32, (CHUNK, CHUNK), 1)
    before = jnp.dot(
        stacked.astype(jnp.bfloat16),
        jnp.where(early < late, 1.0, 0.0).astype(jnp.bfloat16),
        preferred_element_type=jnp.float32,
    )
    diagonal = (
        lax.broadcasted_iota(jnp.int32, (FIBER, FIBER), 0)
        == lax.broadcasted_iota(jnp.int32, (FIBER, FIBER), 1)
    )
    eye = jnp.where(diagonal, 1.0, 0.0).astype(jnp.bfloat16)
    table = jnp.concatenate(
        [f3_ref[:, k * FIBER : (k + 1) * FIBER] for k in range(blocks)], axis=0
    )
    position = lax.broadcasted_iota(jnp.int32, (FIBER, CHUNK), 0)
    kind = lax.broadcasted_iota(jnp.int32, (16, CHUNK), 0)
    carry = jnp.zeros((nf, 1), jnp.float32)
    for k in range(chunks):
        cols = slice(k * CHUNK, (k + 1) * CHUNK)
        mem = member[:, cols]
        rank = jnp.sum(mem * (before[k * nf : (k + 1) * nf] + carry), axis=0, keepdims=True)
        carry = carry + jnp.sum(mem, axis=1, keepdims=True)
        slots[:, cols] = onehot(cap, rank)
        marks = jnp.where(
            kind == 0,
            dest_ref[:, cols],
            jnp.where(
                kind == 1,
                row_ref[:, cols] % br,
                jnp.where(kind == 2, first_ref[:, cols], 0),
            ),
        )
        vals_copy(k).wait()
        turned = dot_nt(eye, vals[cols, :])
        masked = jnp.where(position < count_ref[:, cols], turned, 0.0).astype(jnp.bfloat16)
        every = jnp.dot(table, masked, preferred_element_type=jnp.float32)
        value = every[0:r3]
        for b in range(1, blocks):
            value = jnp.where(block_ref[:, cols] == b, every[b * r3 : (b + 1) * r3], value)
        high = value.astype(jnp.bfloat16)
        low = (value - high.astype(jnp.float32)).astype(jnp.bfloat16)
        data = jnp.concatenate([high, low, marks.astype(jnp.float32).astype(jnp.bfloat16)], axis=0)
        for g in range(nf):
            spread[g * feats : (g + 1) * feats, cols] = data * mem[g : g + 1].astype(jnp.bfloat16)

    share = nf // SPLIT

    def compact(h):
        rows = slice(h * share * feats, (h + 1) * share * feats)
        together = dot_nt(spread[rows, :], slots[...])
        for g in range(share):
            block = together[g * feats : (g + 1) * feats]
            value = block[0:r3] + block[r3 : 2 * r3]
            top = jnp.max(jnp.abs(value), axis=0, keepdims=True)
            scale = jnp.maximum(top, 1e-32) * (1.0 / 32512.0)
            coded = jnp.floor(value * (1.0 / scale) + 0.5).astype(jnp.int32).astype(jnp.int16)
            marks = block[2 * r3 : 2 * r3 + 3]
            key = (marks[0:1] * br + marks[1:2]) * i1 + marks[2:3]
            j = h * share + g
            if j == 0:
                got[0, 0] = coded
                got_key[0, 0, 0:1] = key
                got_key[0, 0, 1:2] = scale
            else:
                send[j] = coded
                send_key[j, 0:1] = key
                send_key[j, 1:2] = scale

    def forward(j):
        for dx in range(1, nx):
            for what in (2, 1, 0):
                x_copy(what, dx, j).start()

    pl.semaphore_wait(barrier, ndev - 1)

    @pl.loop(1, nf)
    def _(j):
        a2a_copy(2, j).start()

    compact(0)

    @pl.loop(1, share)
    def _(j):
        a2a_copy(1, j).start()
        a2a_copy(0, j).start()

    forward(0)
    for h in range(1, SPLIT):
        compact(h)

        @pl.loop(h * share, (h + 1) * share)
        def _(j):
            a2a_copy(1, j).start()
            a2a_copy(0, j).start()

    for dq in range(1, nc):
        f2_copy(dq).start()

    def terms(dx, j):
        key = got_key[dx, j, 0:1]
        target = jnp.floor(key * (1.0 / i1))
        slab = got_f1[j, x] if dx == 0 else got_f1x[dx, j]
        fr = jnp.dot(slab, onehot(i1, key - target * i1), preferred_element_type=jnp.float32)
        sel = onehot(nc * br, target)
        value = got[dx, j].astype(jnp.int32).astype(jnp.float32) * got_key[dx, j, 1:2]
        prod = jnp.concatenate([fr[a : a + 1] * value for a in range(per_x)], axis=0)
        high = prod.astype(jnp.bfloat16)
        low = (prod - high.astype(jnp.float32)).astype(jnp.bfloat16)
        return [high, low], [sel, sel]

    def arrive(which):
        left, right = [], []
        for dx, j in which:
            more_left, more_right = terms(dx, j)
            left += more_left
            right += more_right
        return dot_nt(jnp.concatenate(left, axis=1), jnp.concatenate(right, axis=1))

    acc[...] = jnp.zeros_like(acc)

    def landed(j):
        for what in (2, 1, 0):
            a2a_copy(what, j).wait()
        forward(j)

    @pl.loop(0, nf // 2)
    def _(i):
        pl.when(i > 0)(lambda: landed(2 * i))
        landed(2 * i + 1)
        acc[...] += arrive([(0, 2 * i), (0, 2 * i + 1)])

    for dx in range(1, nx):

        @pl.loop(0, nf // 2)
        def _(i):
            for half in range(2):
                for what in (2, 1, 0):
                    x_copy(what, dx, 2 * i + half).wait()
            acc[...] += arrive([(dx, 2 * i), (dx, 2 * i + 1)])

    def sib_copy(k):
        return pltpu.make_async_remote_copy(
            src_ref=acc.at[pl.ds((1 - c) * quarter + k * LANES, LANES)],
            dst_ref=sib.at[pl.ds(k * LANES, LANES)],
            send_sem=sib_send.at[k],
            recv_sem=sib_recv.at[k],
            device_id=(x * 2 + 1 - c, f),
            device_id_type=MESH,
        )

    def gram_copy(p, to):
        return pltpu.make_async_remote_copy(
            src_ref=gram.at[p],
            dst_ref=grecv.at[f],
            send_sem=g_send,
            recv_sem=g_recv,
            device_id=(q, to),
            device_id_type=MESH,
        )

    def row_copy(dq):
        there = lax.rem(q + dq, nc)
        return pltpu.make_async_remote_copy(
            src_ref=rows_out.at[there],
            dst_ref=rows_in.at[q],
            send_sem=row_send.at[dq],
            recv_sem=row_recv.at[dq],
            device_id=(there, f),
            device_id_type=MESH,
        )

    def back_copy(k, slot):
        to = lax.rem(me + k, ndev)
        return pltpu.make_async_remote_copy(
            src_ref=gown,
            dst_ref=gall.at[slot],
            send_sem=b_send,
            recv_sem=b_recv,
            device_id=(to // nf, lax.rem(to, nf)),
            device_id_type=MESH,
        )

    def drain(ref, count, sem):
        pltpu.make_async_copy(ref.at[pl.ds(0, count)], ref.at[pl.ds(0, count)], sem).wait()

    for k in range(parts):
        sib_copy(k).start()
    for dq in range(1, nc):
        f2_copy(dq).wait()
    second = jnp.concatenate([f2all[k] for k in range(nc)], axis=1)
    totals = []
    for k in range(parts):
        sib_copy(k).wait()
        total = acc[pl.ds(c * quarter + k * LANES, LANES), :] + sib[k * LANES : (k + 1) * LANES, :]
        totals.append(total)
        local = dot_nt(second, total.astype(jnp.bfloat16))
        for h in range(per_part):
            p = k * per_part + h
            to = nf // 4 + p * stride
            piece = local[h * GROWS : (h + 1) * GROWS]
            gram[p] = piece

            @pl.when(f != to)
            def _():
                gram_copy(p, to).start()

            @pl.when(f == to)
            def _():
                grecv[f] = piece

    for k in range(parts):
        upright = totals[k].T.astype(jnp.bfloat16)
        for d in range(nc):
            rows_out[d, :, k * LANES : (k + 1) * LANES] = upright[d * br : (d + 1) * br]
    for dq in range(1, nc):
        row_copy(dq).start()

    shifted = lax.rem(f + nf - nf // 4, nf)
    mine = shifted // stride
    owns = jnp.logical_and(shifted < pieces * stride, lax.rem(shifted, stride) == 0)

    @pl.when(owns)
    def _():
        drain(grecv, nf - 1, g_recv)
        whole = jnp.sum(grecv[...], axis=0).astype(jnp.bfloat16)
        slot = q * pieces + mine
        gown[...] = whole
        gall[slot] = whole

        @pl.loop(1, ndev)
        def _(k):
            back_copy(k, slot).start()

    rows_in[q] = rows_out[q]
    for dq in range(1, nc):
        row_copy(dq).wait()
    for d in range(nc):
        ttmc_ref[:, d * quarter : (d + 1) * quarter] = rows_in[d]

    @pl.when(owns)
    def _():
        drain(gall, nc * pieces - 1, b_recv)

    @pl.when(jnp.logical_not(owns))
    def _():
        drain(gall, nc * pieces, b_recv)

    for d in range(nc):
        for p in range(pieces):
            k, h = p // per_part, p % per_part
            start = d * quarter + k * LANES
            gfull[h * GROWS : (h + 1) * GROWS, start : start + LANES] = gall[d * pieces + p]
    out_ref[...] = dot_nt(gfull[...], ttmc_ref[...]) / 32.0

    @pl.when(owns)
    def _():
        drain(gram, pieces - 1, g_send)
        drain(back, ndev - 1, b_send)

    @pl.when(jnp.logical_not(owns))
    def _():
        drain(gram, pieces, g_send)


def body(
    tile_vals,
    tile_count,
    tile_dest,
    tile_row,
    tile_block,
    tile_first,
    factor_one,
    factor_three,
    factor_two,
):
    nc = lax.axis_size("cuts")
    nf = lax.axis_size("fiber")
    tiles = tile_vals.shape[0]
    r1, r2, r3 = factor_one.shape[1], factor_two.shape[1], factor_three.shape[1]
    br = factor_two.shape[0]
    cap = tiles // nf
    width = r1 * r3
    nx = nc // 2
    i1 = factor_one.shape[0]
    feats = 2 * r3 + 16
    quarter = width // nc
    parts = quarter // LANES
    pieces = parts * (r2 // GROWS)
    vmem = pl.BlockSpec(memory_space=pltpu.VMEM)
    bf16, f32, i16 = jnp.bfloat16, jnp.float32, jnp.int16
    dma = pltpu.SemaphoreType.DMA
    ttmc, projected = pl.pallas_call(
        functools.partial(kernel, nc, nf),
        out_shape=(
            jax.ShapeDtypeStruct((br, width), bf16),
            jax.ShapeDtypeStruct((r2, br), f32),
        ),
        in_specs=[pl.BlockSpec(memory_space=pl.ANY)] + [vmem] * 8,
        out_specs=(vmem, vmem),
        scratch_shapes=[
            pltpu.VMEM((tiles, FIBER), bf16),
            pltpu.VMEM((cap, tiles), bf16),
            pltpu.VMEM((nf * feats, tiles), bf16),
            pltpu.VMEM((nf, r3, cap), i16),
            pltpu.VMEM((nf, 2, cap), f32),
            pltpu.VMEM((nx, nf, r3, cap), i16),
            pltpu.VMEM((nx, nf, 2, cap), f32),
            pltpu.VMEM((nx, r1 // nx, i1), bf16),
            pltpu.VMEM((nf, nx, r1 // nx, i1), bf16),
            pltpu.VMEM((nx, nf, r1 // nx, i1), bf16),
            pltpu.VMEM((nc, r2, br), bf16),
            pltpu.VMEM((width // nx, nc * br), f32),
            pltpu.VMEM((quarter, nc * br), f32),
            pltpu.VMEM((pieces, GROWS, LANES), f32),
            pltpu.VMEM((nf, GROWS, LANES), f32),
            pltpu.VMEM((GROWS, LANES), bf16),
            pltpu.VMEM((nc * pieces, GROWS, LANES), bf16),
            pltpu.VMEM((nc * nf, GROWS, LANES), bf16),
            pltpu.VMEM((r2, width), bf16),
            pltpu.VMEM((nc, br, quarter), bf16),
            pltpu.VMEM((nc, br, quarter), bf16),
            dma((tiles // CHUNK,)),
            dma((3, nf)),
            dma((3, nf)),
            dma((3, nx, nf)),
            dma((3, nx, nf)),
            dma((nc,)),
            dma((nc,)),
            dma((parts,)),
            dma((parts,)),
            dma((nc,)),
            dma((nc,)),
            dma,
            dma,
            dma,
            dma,
        ],
        compiler_params=pltpu.CompilerParams(
            collective_id=0, has_side_effects=True, vmem_limit_bytes=60 * 1024 * 1024
        ),
    )(
        tile_vals,
        tile_count.reshape(1, tiles),
        tile_dest.reshape(1, tiles),
        tile_row.reshape(1, tiles),
        tile_block.reshape(1, tiles),
        tile_first.reshape(1, tiles),
        factor_one.T,
        factor_two.T,
        factor_three.T,
    )
    return ttmc, projected.T


def solution(mesh):
    in_specs = (
        P(("cuts", "fiber"), None),
        P(("cuts", "fiber")),
        P(("cuts", "fiber"), None),
        P(("cuts", "fiber")),
        P(("cuts", "fiber")),
        P(("cuts", "fiber")),
        P(("cuts", "fiber"), None),
        P("fiber", None),
        P(("cuts", "fiber"), None),
    )
    out_specs = (P(("cuts", "fiber"), None), P(("cuts", "fiber"), None))
    return jax.shard_map(body, mesh=mesh, in_specs=in_specs, out_specs=out_specs, check_vma=False)
```

```python
import functools

import jax
import jax.numpy as jnp
from jax import lax
from jax.experimental import pallas as pl
from jax.experimental.pallas import tpu as pltpu
from jax.sharding import PartitionSpec as P

FIBER = 128
CHUNK = 512
LANES = 128
GROWS = 16
SPLIT = 2
LAG = 2
MESH = pl.DeviceIdType.MESH
NT = (((1,), (1,)), ((), ()))


def onehot(count, row, dtype=jnp.bfloat16):
    spots = lax.broadcasted_iota(jnp.int32, (count, row.shape[1]), 0).astype(row.dtype)
    return jnp.where(spots == row, 1.0, 0.0).astype(dtype)


def dot_nt(a, b):
    return lax.dot_general(a, b, NT, preferred_element_type=jnp.float32)


def kernel(
    nc,
    nf,
    vals_hbm,
    count_ref,
    dest_ref,
    row_ref,
    block_ref,
    first_ref,
    f1_ref,
    f2_ref,
    f3_ref,
    ttmc_ref,
    gfull,
    vals,
    slots,
    spread,
    send,
    send_key,
    got,
    got_key,
    f1s,
    got_f1,
    got_f1x,
    f2all,
    acc,
    sib,
    gram,
    grecv,
    gown,
    gall,
    back,
    rows_out,
    rows_in,
    v_sem,
    a2a_send,
    a2a_recv,
    x_send,
    x_recv,
    f2_send,
    f2_recv,
    sib_send,
    sib_recv,
    row_send,
    row_recv,
    g_send,
    g_recv,
    b_send,
    b_recv,
):
    tiles = vals.shape[0]
    r1, i1 = f1_ref.shape
    r2, br = f2_ref.shape
    r3 = f3_ref.shape[0]
    blocks = f3_ref.shape[1] // FIBER
    cap = send.shape[2]
    chunks = tiles // CHUNK
    width = r1 * r3
    nx = nc // 2
    per_x = r1 // nx
    quarter = width // nc
    feats = spread.shape[0] // nf
    ndev = nc * nf
    parts = quarter // LANES
    per_part = r2 // GROWS
    pieces = parts * per_part
    stride = (nf // 2) // pieces
    q = lax.axis_index("cuts")
    f = lax.axis_index("fiber")
    x = q // 2
    c = q % 2
    me = q * nf + f

    def vals_copy(k):
        rows = pl.ds(k * CHUNK, CHUNK)
        return pltpu.make_async_copy(vals_hbm.at[rows], vals.at[rows], v_sem.at[k])

    for k in range(chunks):
        vals_copy(k).start()

    barrier = pltpu.get_barrier_semaphore()

    @pl.loop(1, ndev)
    def _(k):
        other = lax.rem(me + k, ndev)
        pl.semaphore_signal(
            barrier, inc=1, device_id=(other // nf, lax.rem(other, nf)), device_id_type=MESH
        )

    def a2a_copy(what, j):
        source = (send.at[j], send_key.at[j], f1s)[what]
        target = (got.at[0, j], got_key.at[0, j], got_f1.at[j])[what]
        return pltpu.make_async_remote_copy(
            src_ref=source,
            dst_ref=target,
            send_sem=a2a_send.at[what, j],
            recv_sem=a2a_recv.at[what, j],
            device_id=(q, lax.rem(f + j, nf)),
            device_id_type=MESH,
        )

    def x_copy(what, dx, j):
        there = lax.rem(x + dx, nx)
        source = (got.at[0, j], got_key.at[0, j], got_f1.at[j, there])[what]
        target = (got.at[dx, j], got_key.at[dx, j], got_f1x.at[dx, j])[what]
        return pltpu.make_async_remote_copy(
            src_ref=source,
            dst_ref=target,
            send_sem=x_send.at[what, dx, j],
            recv_sem=x_recv.at[what, dx, j],
            device_id=(there * 2 + c, f),
            device_id_type=MESH,
        )

    def f2_copy(dq):
        return pltpu.make_async_remote_copy(
            src_ref=f2all.at[q],
            dst_ref=f2all.at[q],
            send_sem=f2_send.at[dq],
            recv_sem=f2_recv.at[dq],
            device_id=(lax.rem(q + dq, nc), f),
            device_id_type=MESH,
        )

    for k in range(nx):
        f1s[k] = f1_ref[k * per_x : (k + 1) * per_x, :]
        got_f1[0, k] = f1_ref[k * per_x : (k + 1) * per_x, :]
    f2all[q] = f2_ref[...]

    groups = lax.rem(lax.broadcasted_iota(jnp.int32, (nf, tiles), 0) + f, nf)
    owner = row_ref[...] // br
    member = jnp.where(groups == owner, 1.0, 0.0)
    stacked = jnp.concatenate(
        [member[:, k * CHUNK : (k + 1) * CHUNK] for k in range(chunks)], axis=0
    )
    early = lax.broadcasted_iota(jnp.int32, (CHUNK, CHUNK), 0)
    late = lax.broadcasted_iota(jnp.int32, (CHUNK, CHUNK), 1)
    before = jnp.dot(
        stacked.astype(jnp.bfloat16),
        jnp.where(early < late, 1.0, 0.0).astype(jnp.bfloat16),
        preferred_element_type=jnp.float32,
    )
    diagonal = (
        lax.broadcasted_iota(jnp.int32, (FIBER, FIBER), 0)
        == lax.broadcasted_iota(jnp.int32, (FIBER, FIBER), 1)
    )
    eye = jnp.where(diagonal, 1.0, 0.0).astype(jnp.bfloat16)
    table = jnp.concatenate(
        [f3_ref[:, k * FIBER : (k + 1) * FIBER] for k in range(blocks)], axis=0
    )
    position = lax.broadcasted_iota(jnp.int32, (FIBER, CHUNK), 0)
    kind = lax.broadcasted_iota(jnp.int32, (16, CHUNK), 0)
    carry = jnp.zeros((nf, 1), jnp.float32)
    for k in range(chunks):
        cols = slice(k * CHUNK, (k + 1) * CHUNK)
        mem = member[:, cols]
        rank = jnp.sum(mem * (before[k * nf : (k + 1) * nf] + carry), axis=0, keepdims=True)
        carry = carry + jnp.sum(mem, axis=1, keepdims=True)
        slots[:, cols] = onehot(cap, rank)
        marks = jnp.where(
            kind == 0,
            dest_ref[:, cols],
            jnp.where(
                kind == 1,
                row_ref[:, cols] % br,
                jnp.where(kind == 2, first_ref[:, cols], 0),
            ),
        )
        vals_copy(k).wait()
        turned = dot_nt(eye, vals[cols, :])
        masked = jnp.where(position < count_ref[:, cols], turned, 0.0).astype(jnp.bfloat16)
        every = jnp.dot(table, masked, preferred_element_type=jnp.float32)
        value = every[0:r3]
        for b in range(1, blocks):
            value = jnp.where(block_ref[:, cols] == b, every[b * r3 : (b + 1) * r3], value)
        high = value.astype(jnp.bfloat16)
        low = (value - high.astype(jnp.float32)).astype(jnp.bfloat16)
        data = jnp.concatenate([high, low, marks.astype(jnp.float32).astype(jnp.bfloat16)], axis=0)
        for g in range(nf):
            spread[g * feats : (g + 1) * feats, cols] = data * mem[g : g + 1].astype(jnp.bfloat16)

    share = nf // SPLIT

    def compact(h):
        rows = slice(h * share * feats, (h + 1) * share * feats)
        together = dot_nt(spread[rows, :], slots[...])
        for g in range(share):
            block = together[g * feats : (g + 1) * feats]
            value = block[0:r3] + block[r3 : 2 * r3]
            top = jnp.max(jnp.abs(value), axis=0, keepdims=True)
            scale = jnp.maximum(top, 1e-32) * (1.0 / 32512.0)
            coded = jnp.floor(value * (1.0 / scale) + 0.5).astype(jnp.int32).astype(jnp.int16)
            marks = block[2 * r3 : 2 * r3 + 3]
            key = (marks[0:1] * br + marks[1:2]) * i1 + marks[2:3]
            j = h * share + g
            if j == 0:
                got[0, 0] = coded
                got_key[0, 0, 0:1] = key
                got_key[0, 0, 1:2] = scale
            else:
                send[j] = coded
                send_key[j, 0:1] = key
                send_key[j, 1:2] = scale

    def forward(j):
        for dx in range(1, nx):
            for what in (2, 1, 0):
                x_copy(what, dx, j).start()

    pl.semaphore_wait(barrier, ndev - 1)

    @pl.loop(1, nf)
    def _(j):
        a2a_copy(2, j).start()

    compact(0)

    @pl.loop(1, share)
    def _(j):
        a2a_copy(1, j).start()
        a2a_copy(0, j).start()

    forward(0)
    for h in range(1, SPLIT):
        compact(h)

        @pl.loop(h * share, (h + 1) * share)
        def _(j):
            a2a_copy(1, j).start()
            a2a_copy(0, j).start()

    for dq in range(1, nc):
        f2_copy(dq).start()

    def terms(dx, j):
        key = got_key[dx, j, 0:1]
        target = jnp.floor(key * (1.0 / i1))
        slab = got_f1[j, x] if dx == 0 else got_f1x[dx, j]
        fr = jnp.dot(slab, onehot(i1, key - target * i1), preferred_element_type=jnp.float32)
        sel = onehot(nc * br, target)
        value = got[dx, j].astype(jnp.int32).astype(jnp.float32) * got_key[dx, j, 1:2]
        prod = jnp.concatenate([fr[a : a + 1] * value for a in range(per_x)], axis=0)
        high = prod.astype(jnp.bfloat16)
        low = (prod - high.astype(jnp.float32)).astype(jnp.bfloat16)
        return [high, low], [sel, sel]

    def arrive(which):
        left, right = [], []
        for dx, j in which:
            more_left, more_right = terms(dx, j)
            left += more_left
            right += more_right
        return dot_nt(jnp.concatenate(left, axis=1), jnp.concatenate(right, axis=1))

    acc[...] = jnp.zeros_like(acc)

    def landed(j):
        for what in (2, 1, 0):
            a2a_copy(what, j).wait()
        forward(j)

    def crossed(i):
        for dx in range(1, nx):
            for half in range(2):
                for what in (2, 1, 0):
                    x_copy(what, dx, 2 * i + half).wait()
            acc[...] += arrive([(dx, 2 * i), (dx, 2 * i + 1)])

    @pl.loop(0, nf // 2)
    def _(i):
        pl.when(i > 0)(lambda: landed(2 * i))
        landed(2 * i + 1)
        acc[...] += arrive([(0, 2 * i), (0, 2 * i + 1)])
        pl.when(i >= LAG)(lambda: crossed(i - LAG))

    pl.loop(nf // 2 - LAG, nf // 2)(crossed)

    def sib_copy(k):
        return pltpu.make_async_remote_copy(
            src_ref=acc.at[pl.ds((1 - c) * quarter + k * LANES, LANES)],
            dst_ref=sib.at[pl.ds(k * LANES, LANES)],
            send_sem=sib_send.at[k],
            recv_sem=sib_recv.at[k],
            device_id=(x * 2 + 1 - c, f),
            device_id_type=MESH,
        )

    def gram_copy(p, to):
        return pltpu.make_async_remote_copy(
            src_ref=gram.at[p],
            dst_ref=grecv.at[f],
            send_sem=g_send,
            recv_sem=g_recv,
            device_id=(q, to),
            device_id_type=MESH,
        )

    def row_copy(dq):
        there = lax.rem(q + dq, nc)
        return pltpu.make_async_remote_copy(
            src_ref=rows_out.at[there],
            dst_ref=rows_in.at[q],
            send_sem=row_send.at[dq],
            recv_sem=row_recv.at[dq],
            device_id=(there, f),
            device_id_type=MESH,
        )

    def back_copy(k, slot):
        to = lax.rem(me + k, ndev)
        return pltpu.make_async_remote_copy(
            src_ref=gown,
            dst_ref=gall.at[slot],
            send_sem=b_send,
            recv_sem=b_recv,
            device_id=(to // nf, lax.rem(to, nf)),
            device_id_type=MESH,
        )

    def drain(ref, count, sem):
        pltpu.make_async_copy(ref.at[pl.ds(0, count)], ref.at[pl.ds(0, count)], sem).wait()

    for k in range(parts):
        sib_copy(k).start()
    for dq in range(1, nc):
        f2_copy(dq).wait()
    second = jnp.concatenate([f2all[k] for k in range(nc)], axis=1)
    totals = []
    for k in range(parts):
        sib_copy(k).wait()
        total = acc[pl.ds(c * quarter + k * LANES, LANES), :] + sib[k * LANES : (k + 1) * LANES, :]
        totals.append(total)
        local = dot_nt(second, total.astype(jnp.bfloat16))
        for h in range(per_part):
            p = k * per_part + h
            to = nf // 4 + p * stride
            piece = local[h * GROWS : (h + 1) * GROWS]
            gram[p] = piece

            @pl.when(f != to)
            def _():
                gram_copy(p, to).start()

            @pl.when(f == to)
            def _():
                grecv[f] = piece

    for k in range(parts):
        upright = totals[k].T.astype(jnp.bfloat16)
        for d in range(nc):
            rows_out[d, :, k * LANES : (k + 1) * LANES] = upright[d * br : (d + 1) * br]
    for dq in range(1, nc):
        row_copy(dq).start()

    shifted = lax.rem(f + nf - nf // 4, nf)
    mine = shifted // stride
    owns = jnp.logical_and(shifted < pieces * stride, lax.rem(shifted, stride) == 0)

    @pl.when(owns)
    def _():
        drain(grecv, nf - 1, g_recv)
        whole = jnp.sum(grecv[...], axis=0).astype(jnp.bfloat16)
        slot = q * pieces + mine
        gown[...] = whole
        gall[slot] = whole

        @pl.loop(1, ndev)
        def _(k):
            back_copy(k, slot).start()

    rows_in[q] = rows_out[q]
    for dq in range(1, nc):
        row_copy(dq).wait()
    for d in range(nc):
        ttmc_ref[:, d * quarter : (d + 1) * quarter] = rows_in[d]

    @pl.when(owns)
    def _():
        drain(gall, nc * pieces - 1, b_recv)

    @pl.when(jnp.logical_not(owns))
    def _():
        drain(gall, nc * pieces, b_recv)

    for d in range(nc):
        for p in range(pieces):
            k, h = p // per_part, p % per_part
            start = d * quarter + k * LANES
            gfull[h * GROWS : (h + 1) * GROWS, start : start + LANES] = gall[d * pieces + p]

    @pl.when(owns)
    def _():
        drain(gram, pieces - 1, g_send)
        drain(back, ndev - 1, b_send)

    @pl.when(jnp.logical_not(owns))
    def _():
        drain(gram, pieces, g_send)


def finish(rows_ref, gram_ref, ttmc_ref, out_ref):
    ttmc_ref[...] = rows_ref[...]
    out_ref[...] = dot_nt(gram_ref[...], rows_ref[...]) / 32.0


def body(
    tile_vals,
    tile_count,
    tile_dest,
    tile_row,
    tile_block,
    tile_first,
    factor_one,
    factor_three,
    factor_two,
):
    nc = lax.axis_size("cuts")
    nf = lax.axis_size("fiber")
    tiles = tile_vals.shape[0]
    r1, r2, r3 = factor_one.shape[1], factor_two.shape[1], factor_three.shape[1]
    br = factor_two.shape[0]
    cap = tiles // nf
    width = r1 * r3
    nx = nc // 2
    i1 = factor_one.shape[0]
    feats = 2 * r3 + 16
    quarter = width // nc
    parts = quarter // LANES
    pieces = parts * (r2 // GROWS)
    vmem = pl.BlockSpec(memory_space=pltpu.VMEM)
    bf16, f32, i16 = jnp.bfloat16, jnp.float32, jnp.int16
    dma = pltpu.SemaphoreType.DMA
    rows, together = pl.pallas_call(
        functools.partial(kernel, nc, nf),
        out_shape=(
            jax.ShapeDtypeStruct((br, width), bf16),
            jax.ShapeDtypeStruct((r2, width), bf16),
        ),
        in_specs=[pl.BlockSpec(memory_space=pl.ANY)] + [vmem] * 8,
        out_specs=(vmem, vmem),
        scratch_shapes=[
            pltpu.VMEM((tiles, FIBER), bf16),
            pltpu.VMEM((cap, tiles), bf16),
            pltpu.VMEM((nf * feats, tiles), bf16),
            pltpu.VMEM((nf, r3, cap), i16),
            pltpu.VMEM((nf, 2, cap), f32),
            pltpu.VMEM((nx, nf, r3, cap), i16),
            pltpu.VMEM((nx, nf, 2, cap), f32),
            pltpu.VMEM((nx, r1 // nx, i1), bf16),
            pltpu.VMEM((nf, nx, r1 // nx, i1), bf16),
            pltpu.VMEM((nx, nf, r1 // nx, i1), bf16),
            pltpu.VMEM((nc, r2, br), bf16),
            pltpu.VMEM((width // nx, nc * br), f32),
            pltpu.VMEM((quarter, nc * br), f32),
            pltpu.VMEM((pieces, GROWS, LANES), f32),
            pltpu.VMEM((nf, GROWS, LANES), f32),
            pltpu.VMEM((GROWS, LANES), bf16),
            pltpu.VMEM((nc * pieces, GROWS, LANES), bf16),
            pltpu.VMEM((nc * nf, GROWS, LANES), bf16),
            pltpu.VMEM((nc, br, quarter), bf16),
            pltpu.VMEM((nc, br, quarter), bf16),
            dma((tiles // CHUNK,)),
            dma((3, nf)),
            dma((3, nf)),
            dma((3, nx, nf)),
            dma((3, nx, nf)),
            dma((nc,)),
            dma((nc,)),
            dma((parts,)),
            dma((parts,)),
            dma((nc,)),
            dma((nc,)),
            dma,
            dma,
            dma,
            dma,
        ],
        compiler_params=pltpu.CompilerParams(
            collective_id=0, has_side_effects=True, vmem_limit_bytes=60 * 1024 * 1024
        ),
    )(
        tile_vals,
        tile_count.reshape(1, tiles),
        tile_dest.reshape(1, tiles),
        tile_row.reshape(1, tiles),
        tile_block.reshape(1, tiles),
        tile_first.reshape(1, tiles),
        factor_one.T,
        factor_two.T,
        factor_three.T,
    )
    ttmc, projected = pl.pallas_call(
        finish,
        out_shape=(
            jax.ShapeDtypeStruct((br, width), bf16),
            jax.ShapeDtypeStruct((r2, br), f32),
        ),
        in_specs=[vmem] * 2,
        out_specs=(vmem, vmem),
    )(rows, together)
    return ttmc, projected.T


def solution(mesh):
    in_specs = (
        P(("cuts", "fiber"), None),
        P(("cuts", "fiber")),
        P(("cuts", "fiber"), None),
        P(("cuts", "fiber")),
        P(("cuts", "fiber")),
        P(("cuts", "fiber")),
        P(("cuts", "fiber"), None),
        P("fiber", None),
        P(("cuts", "fiber"), None),
    )
    out_specs = (P(("cuts", "fiber"), None), P(("cuts", "fiber"), None))
    return jax.shard_map(body, mesh=mesh, in_specs=in_specs, out_specs=out_specs, check_vma=False)
```

```python
import functools

import jax
import jax.numpy as jnp
from jax import lax
from jax.experimental import pallas as pl
from jax.experimental.pallas import tpu as pltpu
from jax.sharding import PartitionSpec as P

FIBER = 128
CHUNK = 512
LANES = 128
GROWS = 16
SPLIT = 2
LAG = 2
MESH = pl.DeviceIdType.MESH
NT = (((1,), (1,)), ((), ()))


def onehot(count, row, dtype=jnp.bfloat16):
    spots = lax.broadcasted_iota(jnp.int32, (count, row.shape[1]), 0).astype(row.dtype)
    return jnp.where(spots == row, 1.0, 0.0).astype(dtype)


def dot_nt(a, b):
    return lax.dot_general(a, b, NT, preferred_element_type=jnp.float32)


def kernel(
    nc,
    nf,
    vals_hbm,
    count_ref,
    dest_ref,
    row_ref,
    block_ref,
    first_ref,
    f1_ref,
    f2_ref,
    f3_ref,
    ttmc_ref,
    gfull,
    vals,
    slots,
    spread,
    send,
    send_key,
    got,
    got_key,
    f1s,
    got_f1,
    got_f1x,
    f2all,
    acc,
    sib,
    gram,
    grecv,
    gown,
    gall,
    back,
    rows_out,
    rows_in,
    v_sem,
    a2a_send,
    a2a_recv,
    x_send,
    x_recv,
    f2_send,
    f2_recv,
    sib_send,
    sib_recv,
    row_send,
    row_recv,
    g_send,
    g_recv,
    b_send,
    b_recv,
):
    tiles = vals.shape[0]
    r1, i1 = f1_ref.shape
    r2, br = f2_ref.shape
    r3 = f3_ref.shape[0]
    blocks = f3_ref.shape[1] // FIBER
    cap = send.shape[2]
    chunks = tiles // CHUNK
    width = r1 * r3
    nx = nc // 2
    per_x = r1 // nx
    quarter = width // nc
    feats = spread.shape[0] // nf
    ndev = nc * nf
    parts = quarter // LANES
    per_part = r2 // GROWS
    pieces = parts * per_part
    stride = (nf // 2) // pieces
    q = lax.axis_index("cuts")
    f = lax.axis_index("fiber")
    x = q // 2
    c = q % 2
    me = q * nf + f

    def vals_copy(k):
        rows = pl.ds(k * CHUNK, CHUNK)
        return pltpu.make_async_copy(vals_hbm.at[rows], vals.at[rows], v_sem.at[k])

    for k in range(chunks):
        vals_copy(k).start()

    barrier = pltpu.get_barrier_semaphore()

    @pl.loop(1, ndev)
    def _(k):
        other = lax.rem(me + k, ndev)
        pl.semaphore_signal(
            barrier, inc=1, device_id=(other // nf, lax.rem(other, nf)), device_id_type=MESH
        )

    def a2a_copy(what, j):
        source = (send.at[j], send_key.at[j], f1s)[what]
        target = (got.at[0, j], got_key.at[0, j], got_f1.at[j])[what]
        return pltpu.make_async_remote_copy(
            src_ref=source,
            dst_ref=target,
            send_sem=a2a_send.at[what, j],
            recv_sem=a2a_recv.at[what, j],
            device_id=(q, lax.rem(f + j, nf)),
            device_id_type=MESH,
        )

    def x_copy(what, dx, j):
        there = lax.rem(x + dx, nx)
        source = (got.at[0, j], got_key.at[0, j], got_f1.at[j, there])[what]
        target = (got.at[dx, j], got_key.at[dx, j], got_f1x.at[dx, j])[what]
        return pltpu.make_async_remote_copy(
            src_ref=source,
            dst_ref=target,
            send_sem=x_send.at[what, dx, j],
            recv_sem=x_recv.at[what, dx, j],
            device_id=(there * 2 + c, f),
            device_id_type=MESH,
        )

    def f2_copy(dq):
        return pltpu.make_async_remote_copy(
            src_ref=f2all.at[q],
            dst_ref=f2all.at[q],
            send_sem=f2_send.at[dq],
            recv_sem=f2_recv.at[dq],
            device_id=(lax.rem(q + dq, nc), f),
            device_id_type=MESH,
        )

    for k in range(nx):
        f1s[k] = f1_ref[k * per_x : (k + 1) * per_x, :]
        got_f1[0, k] = f1_ref[k * per_x : (k + 1) * per_x, :]
    f2all[q] = f2_ref[...]

    groups = lax.rem(lax.broadcasted_iota(jnp.int32, (nf, tiles), 0) + f, nf)
    owner = row_ref[...] // br
    member = jnp.where(groups == owner, 1.0, 0.0)
    stacked = jnp.concatenate(
        [member[:, k * CHUNK : (k + 1) * CHUNK] for k in range(chunks)], axis=0
    )
    early = lax.broadcasted_iota(jnp.int32, (CHUNK, CHUNK), 0)
    late = lax.broadcasted_iota(jnp.int32, (CHUNK, CHUNK), 1)
    before = jnp.dot(
        stacked.astype(jnp.bfloat16),
        jnp.where(early < late, 1.0, 0.0).astype(jnp.bfloat16),
        preferred_element_type=jnp.float32,
    )
    diagonal = (
        lax.broadcasted_iota(jnp.int32, (FIBER, FIBER), 0)
        == lax.broadcasted_iota(jnp.int32, (FIBER, FIBER), 1)
    )
    eye = jnp.where(diagonal, 1.0, 0.0).astype(jnp.bfloat16)
    table = jnp.concatenate(
        [f3_ref[:, k * FIBER : (k + 1) * FIBER] for k in range(blocks)], axis=0
    )
    position = lax.broadcasted_iota(jnp.int32, (FIBER, CHUNK), 0)
    kind = lax.broadcasted_iota(jnp.int32, (16, CHUNK), 0)
    carry = jnp.zeros((nf, 1), jnp.float32)
    for k in range(chunks):
        cols = slice(k * CHUNK, (k + 1) * CHUNK)
        mem = member[:, cols]
        rank = jnp.sum(mem * (before[k * nf : (k + 1) * nf] + carry), axis=0, keepdims=True)
        carry = carry + jnp.sum(mem, axis=1, keepdims=True)
        slots[:, cols] = onehot(cap, rank)
        marks = jnp.where(
            kind == 0,
            dest_ref[:, cols],
            jnp.where(
                kind == 1,
                row_ref[:, cols] % br,
                jnp.where(kind == 2, first_ref[:, cols], 0),
            ),
        )
        vals_copy(k).wait()
        turned = dot_nt(eye, vals[cols, :])
        masked = jnp.where(position < count_ref[:, cols], turned, 0.0).astype(jnp.bfloat16)
        every = jnp.dot(table, masked, preferred_element_type=jnp.float32)
        value = every[0:r3]
        for b in range(1, blocks):
            value = jnp.where(block_ref[:, cols] == b, every[b * r3 : (b + 1) * r3], value)
        high = value.astype(jnp.bfloat16)
        low = (value - high.astype(jnp.float32)).astype(jnp.bfloat16)
        data = jnp.concatenate([high, low, marks.astype(jnp.float32).astype(jnp.bfloat16)], axis=0)
        for g in range(nf):
            spread[g * feats : (g + 1) * feats, cols] = data * mem[g : g + 1].astype(jnp.bfloat16)

    share = nf // SPLIT

    def compact(h):
        rows = slice(h * share * feats, (h + 1) * share * feats)
        together = dot_nt(spread[rows, :], slots[...])
        for g in range(share):
            block = together[g * feats : (g + 1) * feats]
            value = block[0:r3] + block[r3 : 2 * r3]
            top = jnp.max(jnp.abs(value), axis=0, keepdims=True)
            scale = jnp.maximum(top, 1e-32) * (1.0 / 32512.0)
            coded = jnp.floor(value * (1.0 / scale) + 0.5).astype(jnp.int32).astype(jnp.int16)
            marks = block[2 * r3 : 2 * r3 + 3]
            key = (marks[0:1] * br + marks[1:2]) * i1 + marks[2:3]
            j = h * share + g
            if j == 0:
                got[0, 0] = coded
                got_key[0, 0, 0:1] = key
                got_key[0, 0, 1:2] = scale
            else:
                send[j] = coded
                send_key[j, 0:1] = key
                send_key[j, 1:2] = scale

    def forward(j):
        for dx in range(1, nx):
            for what in (2, 1, 0):
                x_copy(what, dx, j).start()

    pl.semaphore_wait(barrier, ndev - 1)

    @pl.loop(1, share)
    def _(j):
        a2a_copy(2, j).start()

    compact(0)

    @pl.loop(1, share)
    def _(j):
        a2a_copy(1, j).start()
        a2a_copy(0, j).start()

    forward(0)

    @pl.loop(share, nf)
    def _(j):
        a2a_copy(2, j).start()

    for h in range(1, SPLIT):
        compact(h)

        @pl.loop(h * share, (h + 1) * share)
        def _(j):
            a2a_copy(1, j).start()
            a2a_copy(0, j).start()

    for dq in range(1, nc):
        f2_copy(dq).start()

    def terms(dx, j):
        key = got_key[dx, j, 0:1]
        target = jnp.floor(key * (1.0 / i1))
        slab = got_f1[j, x] if dx == 0 else got_f1x[dx, j]
        fr = jnp.dot(slab, onehot(i1, key - target * i1), preferred_element_type=jnp.float32)
        sel = onehot(nc * br, target)
        value = got[dx, j].astype(jnp.int32).astype(jnp.float32) * got_key[dx, j, 1:2]
        prod = jnp.concatenate([fr[a : a + 1] * value for a in range(per_x)], axis=0)
        high = prod.astype(jnp.bfloat16)
        low = (prod - high.astype(jnp.float32)).astype(jnp.bfloat16)
        return [high, low], [sel, sel]

    def arrive(which):
        left, right = [], []
        for dx, j in which:
            more_left, more_right = terms(dx, j)
            left += more_left
            right += more_right
        return dot_nt(jnp.concatenate(left, axis=1), jnp.concatenate(right, axis=1))

    acc[...] = jnp.zeros_like(acc)

    def landed(j):
        for what in (2, 1, 0):
            a2a_copy(what, j).wait_recv()
        forward(j)

    def crossed(i):
        for dx in range(1, nx):
            for half in range(2):
                for what in (2, 1, 0):
                    x_copy(what, dx, 2 * i + half).wait_recv()
            acc[...] += arrive([(dx, 2 * i), (dx, 2 * i + 1)])

    @pl.loop(0, nf // 2)
    def _(i):
        pl.when(i > 0)(lambda: landed(2 * i))
        landed(2 * i + 1)
        acc[...] += arrive([(0, 2 * i), (0, 2 * i + 1)])
        pl.when(i >= LAG)(lambda: crossed(i - LAG))

    pl.loop(nf // 2 - LAG, nf // 2)(crossed)

    def sib_copy(k):
        return pltpu.make_async_remote_copy(
            src_ref=acc.at[pl.ds((1 - c) * quarter + k * LANES, LANES)],
            dst_ref=sib.at[pl.ds(k * LANES, LANES)],
            send_sem=sib_send.at[k],
            recv_sem=sib_recv.at[k],
            device_id=(x * 2 + 1 - c, f),
            device_id_type=MESH,
        )

    def gram_copy(p, to):
        return pltpu.make_async_remote_copy(
            src_ref=gram.at[p],
            dst_ref=grecv.at[f],
            send_sem=g_send,
            recv_sem=g_recv,
            device_id=(q, to),
            device_id_type=MESH,
        )

    def row_copy(dq):
        there = lax.rem(q + dq, nc)
        return pltpu.make_async_remote_copy(
            src_ref=rows_out.at[there],
            dst_ref=rows_in.at[q],
            send_sem=row_send.at[dq],
            recv_sem=row_recv.at[dq],
            device_id=(there, f),
            device_id_type=MESH,
        )

    def back_copy(k, slot):
        to = lax.rem(me + k, ndev)
        return pltpu.make_async_remote_copy(
            src_ref=gown,
            dst_ref=gall.at[slot],
            send_sem=b_send,
            recv_sem=b_recv,
            device_id=(to // nf, lax.rem(to, nf)),
            device_id_type=MESH,
        )

    def drain(ref, count, sem):
        pltpu.make_async_copy(ref.at[pl.ds(0, count)], ref.at[pl.ds(0, count)], sem).wait()

    for k in range(parts):
        sib_copy(k).start()
    for dq in range(1, nc):
        f2_copy(dq).wait_recv()
    second = jnp.concatenate([f2all[k] for k in range(nc)], axis=1)
    totals = []
    for k in range(parts):
        sib_copy(k).wait_recv()
        total = acc[pl.ds(c * quarter + k * LANES, LANES), :] + sib[k * LANES : (k + 1) * LANES, :]
        totals.append(total)
        local = dot_nt(second, total.astype(jnp.bfloat16))
        for h in range(per_part):
            p = k * per_part + h
            to = nf // 4 + p * stride
            piece = local[h * GROWS : (h + 1) * GROWS]
            gram[p] = piece

            @pl.when(f != to)
            def _():
                gram_copy(p, to).start()

            @pl.when(f == to)
            def _():
                grecv[f] = piece

    for k in range(parts):
        upright = totals[k].T.astype(jnp.bfloat16)
        for d in range(nc):
            rows_out[d, :, k * LANES : (k + 1) * LANES] = upright[d * br : (d + 1) * br]
    for dq in range(1, nc):
        row_copy(dq).start()

    shifted = lax.rem(f + nf - nf // 4, nf)
    mine = shifted // stride
    owns = jnp.logical_and(shifted < pieces * stride, lax.rem(shifted, stride) == 0)

    @pl.when(owns)
    def _():
        drain(grecv, nf - 1, g_recv)
        whole = jnp.sum(grecv[...], axis=0).astype(jnp.bfloat16)
        slot = q * pieces + mine
        gown[...] = whole
        gall[slot] = whole

        @pl.loop(1, ndev)
        def _(k):
            back_copy(k, slot).start()

    rows_in[q] = rows_out[q]
    for dq in range(1, nc):
        row_copy(dq).wait_recv()
    for d in range(nc):
        ttmc_ref[:, d * quarter : (d + 1) * quarter] = rows_in[d]

    @pl.loop(0, nf)
    def _(j):
        @pl.when(j > 0)
        def _():
            for what in range(3):
                a2a_copy(what, j).wait_send()

        for dx in range(1, nx):
            for what in range(3):
                x_copy(what, dx, j).wait_send()

    for dq in range(1, nc):
        f2_copy(dq).wait_send()
        row_copy(dq).wait_send()
    for k in range(parts):
        sib_copy(k).wait_send()

    @pl.when(owns)
    def _():
        drain(gall, nc * pieces - 1, b_recv)

    @pl.when(jnp.logical_not(owns))
    def _():
        drain(gall, nc * pieces, b_recv)

    for d in range(nc):
        for p in range(pieces):
            k, h = p // per_part, p % per_part
            start = d * quarter + k * LANES
            gfull[h * GROWS : (h + 1) * GROWS, start : start + LANES] = gall[d * pieces + p]

    @pl.when(owns)
    def _():
        drain(gram, pieces - 1, g_send)
        drain(back, ndev - 1, b_send)

    @pl.when(jnp.logical_not(owns))
    def _():
        drain(gram, pieces, g_send)


def finish(rows_ref, gram_ref, ttmc_ref, out_ref):
    ttmc_ref[...] = rows_ref[...]
    out_ref[...] = dot_nt(gram_ref[...], rows_ref[...]) / 32.0


def body(
    tile_vals,
    tile_count,
    tile_dest,
    tile_row,
    tile_block,
    tile_first,
    factor_one,
    factor_three,
    factor_two,
):
    nc = lax.axis_size("cuts")
    nf = lax.axis_size("fiber")
    tiles = tile_vals.shape[0]
    r1, r2, r3 = factor_one.shape[1], factor_two.shape[1], factor_three.shape[1]
    br = factor_two.shape[0]
    cap = tiles // nf
    width = r1 * r3
    nx = nc // 2
    i1 = factor_one.shape[0]
    feats = 2 * r3 + 16
    quarter = width // nc
    parts = quarter // LANES
    pieces = parts * (r2 // GROWS)
    vmem = pl.BlockSpec(memory_space=pltpu.VMEM)
    bf16, f32, i16 = jnp.bfloat16, jnp.float32, jnp.int16
    dma = pltpu.SemaphoreType.DMA
    rows, together = pl.pallas_call(
        functools.partial(kernel, nc, nf),
        out_shape=(
            jax.ShapeDtypeStruct((br, width), bf16),
            jax.ShapeDtypeStruct((r2, width), bf16),
        ),
        in_specs=[pl.BlockSpec(memory_space=pl.ANY)] + [vmem] * 8,
        out_specs=(vmem, vmem),
        scratch_shapes=[
            pltpu.VMEM((tiles, FIBER), bf16),
            pltpu.VMEM((cap, tiles), bf16),
            pltpu.VMEM((nf * feats, tiles), bf16),
            pltpu.VMEM((nf, r3, cap), i16),
            pltpu.VMEM((nf, 2, cap), f32),
            pltpu.VMEM((nx, nf, r3, cap), i16),
            pltpu.VMEM((nx, nf, 2, cap), f32),
            pltpu.VMEM((nx, r1 // nx, i1), bf16),
            pltpu.VMEM((nf, nx, r1 // nx, i1), bf16),
            pltpu.VMEM((nx, nf, r1 // nx, i1), bf16),
            pltpu.VMEM((nc, r2, br), bf16),
            pltpu.VMEM((width // nx, nc * br), f32),
            pltpu.VMEM((quarter, nc * br), f32),
            pltpu.VMEM((pieces, GROWS, LANES), f32),
            pltpu.VMEM((nf, GROWS, LANES), f32),
            pltpu.VMEM((GROWS, LANES), bf16),
            pltpu.VMEM((nc * pieces, GROWS, LANES), bf16),
            pltpu.VMEM((nc * nf, GROWS, LANES), bf16),
            pltpu.VMEM((nc, br, quarter), bf16),
            pltpu.VMEM((nc, br, quarter), bf16),
            dma((tiles // CHUNK,)),
            dma((3, nf)),
            dma((3, nf)),
            dma((3, nx, nf)),
            dma((3, nx, nf)),
            dma((nc,)),
            dma((nc,)),
            dma((parts,)),
            dma((parts,)),
            dma((nc,)),
            dma((nc,)),
            dma,
            dma,
            dma,
            dma,
        ],
        compiler_params=pltpu.CompilerParams(
            collective_id=0, has_side_effects=True, vmem_limit_bytes=60 * 1024 * 1024
        ),
    )(
        tile_vals,
        tile_count.reshape(1, tiles),
        tile_dest.reshape(1, tiles),
        tile_row.reshape(1, tiles),
        tile_block.reshape(1, tiles),
        tile_first.reshape(1, tiles),
        factor_one.T,
        factor_two.T,
        factor_three.T,
    )
    ttmc, projected = pl.pallas_call(
        finish,
        out_shape=(
            jax.ShapeDtypeStruct((br, width), bf16),
            jax.ShapeDtypeStruct((r2, br), f32),
        ),
        in_specs=[vmem] * 2,
        out_specs=(vmem, vmem),
    )(rows, together)
    return ttmc, projected.T


def solution(mesh):
    in_specs = (
        P(("cuts", "fiber"), None),
        P(("cuts", "fiber")),
        P(("cuts", "fiber"), None),
        P(("cuts", "fiber")),
        P(("cuts", "fiber")),
        P(("cuts", "fiber")),
        P(("cuts", "fiber"), None),
        P("fiber", None),
        P(("cuts", "fiber"), None),
    )
    out_specs = (P(("cuts", "fiber"), None), P(("cuts", "fiber"), None))
    return jax.shard_map(body, mesh=mesh, in_specs=in_specs, out_specs=out_specs, check_vma=False)
```

```python
import functools

import jax
import jax.numpy as jnp
from jax import lax
from jax.experimental import pallas as pl
from jax.experimental.pallas import tpu as pltpu
from jax.sharding import PartitionSpec as P

FIBER = 128
CHUNK = 512
LANES = 128
GROWS = 16
SPLIT = 2
LAG = 2
MESH = pl.DeviceIdType.MESH
NT = (((1,), (1,)), ((), ()))


def onehot(count, row, dtype=jnp.bfloat16):
    spots = lax.broadcasted_iota(jnp.int32, (count, row.shape[1]), 0).astype(row.dtype)
    return jnp.where(spots == row, 1.0, 0.0).astype(dtype)


def dot_nt(a, b):
    return lax.dot_general(a, b, NT, preferred_element_type=jnp.float32)


def kernel(
    nc,
    nf,
    vals_hbm,
    count_ref,
    dest_ref,
    row_ref,
    block_ref,
    first_ref,
    f1_ref,
    f2_ref,
    f3_ref,
    ttmc_hbm,
    gfull,
    ttmc_ref,
    vals,
    slots,
    spread,
    send,
    send_key,
    got,
    got_key,
    f1s,
    got_f1,
    got_f1x,
    f2all,
    acc,
    sib,
    gram,
    grecv,
    gown,
    gall,
    back,
    rows_out,
    rows_in,
    v_sem,
    out_sem,
    a2a_send,
    a2a_recv,
    x_send,
    x_recv,
    f2_send,
    f2_recv,
    sib_send,
    sib_recv,
    row_send,
    row_recv,
    g_send,
    g_recv,
    b_send,
    b_recv,
):
    tiles = vals.shape[0]
    r1, i1 = f1_ref.shape
    r2, br = f2_ref.shape
    r3 = f3_ref.shape[0]
    blocks = f3_ref.shape[1] // FIBER
    cap = send.shape[2]
    chunks = tiles // CHUNK
    width = r1 * r3
    nx = nc // 2
    per_x = r1 // nx
    quarter = width // nc
    feats = spread.shape[0] // nf
    ndev = nc * nf
    parts = quarter // LANES
    per_part = r2 // GROWS
    pieces = parts * per_part
    stride = (nf // 2) // pieces
    q = lax.axis_index("cuts")
    f = lax.axis_index("fiber")
    x = q // 2
    c = q % 2
    me = q * nf + f

    def vals_copy(k):
        rows = pl.ds(k * CHUNK, CHUNK)
        return pltpu.make_async_copy(vals_hbm.at[rows], vals.at[rows], v_sem.at[k])

    for k in range(chunks):
        vals_copy(k).start()

    barrier = pltpu.get_barrier_semaphore()

    @pl.loop(1, ndev)
    def _(k):
        other = lax.rem(me + k, ndev)
        pl.semaphore_signal(
            barrier, inc=1, device_id=(other // nf, lax.rem(other, nf)), device_id_type=MESH
        )

    def a2a_copy(what, j):
        source = (send.at[j], send_key.at[j], f1s)[what]
        target = (got.at[0, j], got_key.at[0, j], got_f1.at[j])[what]
        return pltpu.make_async_remote_copy(
            src_ref=source,
            dst_ref=target,
            send_sem=a2a_send.at[what, j],
            recv_sem=a2a_recv.at[what, j],
            device_id=(q, lax.rem(f + j, nf)),
            device_id_type=MESH,
        )

    def x_copy(what, dx, j):
        there = lax.rem(x + dx, nx)
        source = (got.at[0, j], got_key.at[0, j], got_f1.at[j, there])[what]
        target = (got.at[dx, j], got_key.at[dx, j], got_f1x.at[dx, j])[what]
        return pltpu.make_async_remote_copy(
            src_ref=source,
            dst_ref=target,
            send_sem=x_send.at[what, dx, j],
            recv_sem=x_recv.at[what, dx, j],
            device_id=(there * 2 + c, f),
            device_id_type=MESH,
        )

    def f2_copy(dq):
        return pltpu.make_async_remote_copy(
            src_ref=f2all.at[q],
            dst_ref=f2all.at[q],
            send_sem=f2_send.at[dq],
            recv_sem=f2_recv.at[dq],
            device_id=(lax.rem(q + dq, nc), f),
            device_id_type=MESH,
        )

    for k in range(nx):
        f1s[k] = f1_ref[k * per_x : (k + 1) * per_x, :]
        got_f1[0, k] = f1_ref[k * per_x : (k + 1) * per_x, :]
    f2all[q] = f2_ref[...]

    groups = lax.rem(lax.broadcasted_iota(jnp.int32, (nf, tiles), 0) + f, nf)
    owner = row_ref[...] // br
    member = jnp.where(groups == owner, 1.0, 0.0)
    stacked = jnp.concatenate(
        [member[:, k * CHUNK : (k + 1) * CHUNK] for k in range(chunks)], axis=0
    )
    early = lax.broadcasted_iota(jnp.int32, (CHUNK, CHUNK), 0)
    late = lax.broadcasted_iota(jnp.int32, (CHUNK, CHUNK), 1)
    before = jnp.dot(
        stacked.astype(jnp.bfloat16),
        jnp.where(early < late, 1.0, 0.0).astype(jnp.bfloat16),
        preferred_element_type=jnp.float32,
    )
    diagonal = (
        lax.broadcasted_iota(jnp.int32, (FIBER, FIBER), 0)
        == lax.broadcasted_iota(jnp.int32, (FIBER, FIBER), 1)
    )
    eye = jnp.where(diagonal, 1.0, 0.0).astype(jnp.bfloat16)
    table = jnp.concatenate(
        [f3_ref[:, k * FIBER : (k + 1) * FIBER] for k in range(blocks)], axis=0
    )
    position = lax.broadcasted_iota(jnp.int32, (FIBER, CHUNK), 0)
    kind = lax.broadcasted_iota(jnp.int32, (16, CHUNK), 0)
    carry = jnp.zeros((nf, 1), jnp.float32)
    for k in range(chunks):
        cols = slice(k * CHUNK, (k + 1) * CHUNK)
        mem = member[:, cols]
        rank = jnp.sum(mem * (before[k * nf : (k + 1) * nf] + carry), axis=0, keepdims=True)
        carry = carry + jnp.sum(mem, axis=1, keepdims=True)
        slots[:, cols] = onehot(cap, rank)
        marks = jnp.where(
            kind == 0,
            dest_ref[:, cols],
            jnp.where(
                kind == 1,
                row_ref[:, cols] % br,
                jnp.where(kind == 2, first_ref[:, cols], 0),
            ),
        )
        vals_copy(k).wait()
        turned = dot_nt(eye, vals[cols, :])
        masked = jnp.where(position < count_ref[:, cols], turned, 0.0).astype(jnp.bfloat16)
        every = jnp.dot(table, masked, preferred_element_type=jnp.float32)
        value = every[0:r3]
        for b in range(1, blocks):
            value = jnp.where(block_ref[:, cols] == b, every[b * r3 : (b + 1) * r3], value)
        high = value.astype(jnp.bfloat16)
        low = (value - high.astype(jnp.float32)).astype(jnp.bfloat16)
        data = jnp.concatenate([high, low, marks.astype(jnp.float32).astype(jnp.bfloat16)], axis=0)
        for g in range(nf):
            spread[g * feats : (g + 1) * feats, cols] = data * mem[g : g + 1].astype(jnp.bfloat16)

    share = nf // SPLIT

    def compact(h):
        rows = slice(h * share * feats, (h + 1) * share * feats)
        together = dot_nt(spread[rows, :], slots[...])
        for g in range(share):
            block = together[g * feats : (g + 1) * feats]
            value = block[0:r3] + block[r3 : 2 * r3]
            top = jnp.max(jnp.abs(value), axis=0, keepdims=True)
            scale = jnp.maximum(top, 1e-32) * (1.0 / 32512.0)
            coded = jnp.floor(value * (1.0 / scale) + 0.5).astype(jnp.int32).astype(jnp.int16)
            marks = block[2 * r3 : 2 * r3 + 3]
            key = (marks[0:1] * br + marks[1:2]) * i1 + marks[2:3]
            j = h * share + g
            if j == 0:
                got[0, 0] = coded
                got_key[0, 0, 0:1] = key
                got_key[0, 0, 1:2] = scale
            else:
                send[j] = coded
                send_key[j, 0:1] = key
                send_key[j, 1:2] = scale

    def forward(j):
        for dx in range(1, nx):
            for what in (2, 1, 0):
                x_copy(what, dx, j).start()

    pl.semaphore_wait(barrier, ndev - 1)

    @pl.loop(1, share)
    def _(j):
        a2a_copy(2, j).start()

    compact(0)

    @pl.loop(1, share)
    def _(j):
        a2a_copy(1, j).start()
        a2a_copy(0, j).start()

    forward(0)

    @pl.loop(share, nf)
    def _(j):
        a2a_copy(2, j).start()

    for h in range(1, SPLIT):
        compact(h)

        @pl.loop(h * share, (h + 1) * share)
        def _(j):
            a2a_copy(1, j).start()
            a2a_copy(0, j).start()

    for dq in range(1, nc):
        f2_copy(dq).start()

    def terms(dx, j):
        key = got_key[dx, j, 0:1]
        target = jnp.floor(key * (1.0 / i1))
        slab = got_f1[j, x] if dx == 0 else got_f1x[dx, j]
        fr = jnp.dot(slab, onehot(i1, key - target * i1), preferred_element_type=jnp.float32)
        sel = onehot(nc * br, target)
        value = got[dx, j].astype(jnp.int32).astype(jnp.float32) * got_key[dx, j, 1:2]
        prod = jnp.concatenate([fr[a : a + 1] * value for a in range(per_x)], axis=0)
        high = prod.astype(jnp.bfloat16)
        low = (prod - high.astype(jnp.float32)).astype(jnp.bfloat16)
        return [high, low], [sel, sel]

    def arrive(which):
        left, right = [], []
        for dx, j in which:
            more_left, more_right = terms(dx, j)
            left += more_left
            right += more_right
        return dot_nt(jnp.concatenate(left, axis=1), jnp.concatenate(right, axis=1))

    acc[...] = jnp.zeros_like(acc)

    def landed(j):
        for what in (2, 1, 0):
            a2a_copy(what, j).wait_recv()
        forward(j)

    def crossed(i):
        for dx in range(1, nx):
            for half in range(2):
                for what in (2, 1, 0):
                    x_copy(what, dx, 2 * i + half).wait_recv()
            acc[...] += arrive([(dx, 2 * i), (dx, 2 * i + 1)])

    @pl.loop(0, nf // 2)
    def _(i):
        pl.when(i > 0)(lambda: landed(2 * i))
        landed(2 * i + 1)
        acc[...] += arrive([(0, 2 * i), (0, 2 * i + 1)])
        pl.when(i >= LAG)(lambda: crossed(i - LAG))

    pl.loop(nf // 2 - LAG, nf // 2)(crossed)

    def sib_copy(k):
        return pltpu.make_async_remote_copy(
            src_ref=acc.at[pl.ds((1 - c) * quarter + k * LANES, LANES)],
            dst_ref=sib.at[pl.ds(k * LANES, LANES)],
            send_sem=sib_send.at[k],
            recv_sem=sib_recv.at[k],
            device_id=(x * 2 + 1 - c, f),
            device_id_type=MESH,
        )

    def gram_copy(p, to):
        return pltpu.make_async_remote_copy(
            src_ref=gram.at[p],
            dst_ref=grecv.at[f],
            send_sem=g_send,
            recv_sem=g_recv,
            device_id=(q, to),
            device_id_type=MESH,
        )

    def row_copy(dq):
        there = lax.rem(q + dq, nc)
        return pltpu.make_async_remote_copy(
            src_ref=rows_out.at[there],
            dst_ref=rows_in.at[q],
            send_sem=row_send.at[dq],
            recv_sem=row_recv.at[dq],
            device_id=(there, f),
            device_id_type=MESH,
        )

    def back_copy(k, slot):
        to = lax.rem(me + k, ndev)
        return pltpu.make_async_remote_copy(
            src_ref=gown,
            dst_ref=gall.at[slot],
            send_sem=b_send,
            recv_sem=b_recv,
            device_id=(to // nf, lax.rem(to, nf)),
            device_id_type=MESH,
        )

    def drain(ref, count, sem):
        pltpu.make_async_copy(ref.at[pl.ds(0, count)], ref.at[pl.ds(0, count)], sem).wait()

    for k in range(parts):
        sib_copy(k).start()
    for dq in range(1, nc):
        f2_copy(dq).wait_recv()
    second = jnp.concatenate([f2all[k] for k in range(nc)], axis=1)
    totals = []
    for k in range(parts):
        sib_copy(k).wait_recv()
        total = acc[pl.ds(c * quarter + k * LANES, LANES), :] + sib[k * LANES : (k + 1) * LANES, :]
        totals.append(total)
        local = dot_nt(second, total.astype(jnp.bfloat16))
        for h in range(per_part):
            p = k * per_part + h
            to = nf // 4 + p * stride
            piece = local[h * GROWS : (h + 1) * GROWS]
            gram[p] = piece

            @pl.when(f != to)
            def _():
                gram_copy(p, to).start()

            @pl.when(f == to)
            def _():
                grecv[f] = piece

    for k in range(parts):
        upright = totals[k].T.astype(jnp.bfloat16)
        for d in range(nc):
            rows_out[d, :, k * LANES : (k + 1) * LANES] = upright[d * br : (d + 1) * br]
    for dq in range(1, nc):
        row_copy(dq).start()

    shifted = lax.rem(f + nf - nf // 4, nf)
    mine = shifted // stride
    owns = jnp.logical_and(shifted < pieces * stride, lax.rem(shifted, stride) == 0)

    @pl.when(owns)
    def _():
        drain(grecv, nf - 1, g_recv)
        whole = jnp.sum(grecv[...], axis=0).astype(jnp.bfloat16)
        slot = q * pieces + mine
        gown[...] = whole
        gall[slot] = whole

        @pl.loop(1, ndev)
        def _(k):
            back_copy(k, slot).start()

    rows_in[q] = rows_out[q]
    for dq in range(1, nc):
        row_copy(dq).wait_recv()
    for d in range(nc):
        ttmc_ref[:, d * quarter : (d + 1) * quarter] = rows_in[d]
    leave = pltpu.make_async_copy(ttmc_ref, ttmc_hbm, out_sem)
    leave.start()

    @pl.loop(0, nf)
    def _(j):
        @pl.when(j > 0)
        def _():
            for what in range(3):
                a2a_copy(what, j).wait_send()

        for dx in range(1, nx):
            for what in range(3):
                x_copy(what, dx, j).wait_send()

    for dq in range(1, nc):
        f2_copy(dq).wait_send()
        row_copy(dq).wait_send()
    for k in range(parts):
        sib_copy(k).wait_send()

    @pl.when(owns)
    def _():
        drain(gall, nc * pieces - 1, b_recv)

    @pl.when(jnp.logical_not(owns))
    def _():
        drain(gall, nc * pieces, b_recv)

    for d in range(nc):
        for p in range(pieces):
            k, h = p // per_part, p % per_part
            start = d * quarter + k * LANES
            gfull[h * GROWS : (h + 1) * GROWS, start : start + LANES] = gall[d * pieces + p]
    leave.wait()

    @pl.when(owns)
    def _():
        drain(gram, pieces - 1, g_send)
        drain(back, ndev - 1, b_send)

    @pl.when(jnp.logical_not(owns))
    def _():
        drain(gram, pieces, g_send)


def finish(rows_ref, gram_ref, ttmc_ref, out_ref):
    ttmc_ref[...] = rows_ref[...]
    out_ref[...] = dot_nt(gram_ref[...], rows_ref[...]) / 32.0


def body(
    tile_vals,
    tile_count,
    tile_dest,
    tile_row,
    tile_block,
    tile_first,
    factor_one,
    factor_three,
    factor_two,
):
    nc = lax.axis_size("cuts")
    nf = lax.axis_size("fiber")
    tiles = tile_vals.shape[0]
    r1, r2, r3 = factor_one.shape[1], factor_two.shape[1], factor_three.shape[1]
    br = factor_two.shape[0]
    cap = tiles // nf
    width = r1 * r3
    nx = nc // 2
    i1 = factor_one.shape[0]
    feats = 2 * r3 + 16
    quarter = width // nc
    parts = quarter // LANES
    pieces = parts * (r2 // GROWS)
    vmem = pl.BlockSpec(memory_space=pltpu.VMEM)
    bf16, f32, i16 = jnp.bfloat16, jnp.float32, jnp.int16
    dma = pltpu.SemaphoreType.DMA
    rows, together = pl.pallas_call(
        functools.partial(kernel, nc, nf),
        out_shape=(
            jax.ShapeDtypeStruct((br, width), bf16),
            jax.ShapeDtypeStruct((r2, width), bf16),
        ),
        in_specs=[pl.BlockSpec(memory_space=pl.ANY)] + [vmem] * 8,
        out_specs=(pl.BlockSpec(memory_space=pl.ANY), vmem),
        scratch_shapes=[
            pltpu.VMEM((br, width), bf16),
            pltpu.VMEM((tiles, FIBER), bf16),
            pltpu.VMEM((cap, tiles), bf16),
            pltpu.VMEM((nf * feats, tiles), bf16),
            pltpu.VMEM((nf, r3, cap), i16),
            pltpu.VMEM((nf, 2, cap), f32),
            pltpu.VMEM((nx, nf, r3, cap), i16),
            pltpu.VMEM((nx, nf, 2, cap), f32),
            pltpu.VMEM((nx, r1 // nx, i1), bf16),
            pltpu.VMEM((nf, nx, r1 // nx, i1), bf16),
            pltpu.VMEM((nx, nf, r1 // nx, i1), bf16),
            pltpu.VMEM((nc, r2, br), bf16),
            pltpu.VMEM((width // nx, nc * br), f32),
            pltpu.VMEM((quarter, nc * br), f32),
            pltpu.VMEM((pieces, GROWS, LANES), f32),
            pltpu.VMEM((nf, GROWS, LANES), f32),
            pltpu.VMEM((GROWS, LANES), bf16),
            pltpu.VMEM((nc * pieces, GROWS, LANES), bf16),
            pltpu.VMEM((nc * nf, GROWS, LANES), bf16),
            pltpu.VMEM((nc, br, quarter), bf16),
            pltpu.VMEM((nc, br, quarter), bf16),
            dma((tiles // CHUNK,)),
            dma,
            dma((3, nf)),
            dma((3, nf)),
            dma((3, nx, nf)),
            dma((3, nx, nf)),
            dma((nc,)),
            dma((nc,)),
            dma((parts,)),
            dma((parts,)),
            dma((nc,)),
            dma((nc,)),
            dma,
            dma,
            dma,
            dma,
        ],
        compiler_params=pltpu.CompilerParams(
            collective_id=0, has_side_effects=True, vmem_limit_bytes=60 * 1024 * 1024
        ),
    )(
        tile_vals,
        tile_count.reshape(1, tiles),
        tile_dest.reshape(1, tiles),
        tile_row.reshape(1, tiles),
        tile_block.reshape(1, tiles),
        tile_first.reshape(1, tiles),
        factor_one.T,
        factor_two.T,
        factor_three.T,
    )
    ttmc, projected = pl.pallas_call(
        finish,
        out_shape=(
            jax.ShapeDtypeStruct((br, width), bf16),
            jax.ShapeDtypeStruct((r2, br), f32),
        ),
        in_specs=[vmem] * 2,
        out_specs=(vmem, vmem),
    )(rows, together)
    return ttmc, projected.T


def solution(mesh):
    in_specs = (
        P(("cuts", "fiber"), None),
        P(("cuts", "fiber")),
        P(("cuts", "fiber"), None),
        P(("cuts", "fiber")),
        P(("cuts", "fiber")),
        P(("cuts", "fiber")),
        P(("cuts", "fiber"), None),
        P("fiber", None),
        P(("cuts", "fiber"), None),
    )
    out_specs = (P(("cuts", "fiber"), None), P(("cuts", "fiber"), None))
    return jax.shard_map(body, mesh=mesh, in_specs=in_specs, out_specs=out_specs, check_vma=False)
```
